32 devices in a mesh: shard: 16 (over z, x, core), replica: 2 (over y).
Axes of the slice: x: 2, y: 2, z: 4, core: 2. Of those that a mesh axis runs over, the one named last changes fastest.
Arguments:
- tokens: float32 [4096, 1024], P(('shard', 'replica')), may hold values from -6 to 6
- segment_ids: int32 [32, 128], P(('shard', 'replica')), may hold values from 0 to 3, never falling along the last dimension, each value on 1 to 64 neighbouring positions
- cotangent: float32 [4096, 1024], P(('shard', 'replica')), may hold values from -6 to 6
- norm1_gain: bfloat16 [1024], P('shard'), may hold values from 0.099609375 to 1.8984375
- norm1_shift: bfloat16 [1024], P('shard'), may hold values from -3 to 3
- qkv_weight: bfloat16 [1024, 3072], P('shard'), may hold values from -0.1875 to 0.1875
- query_bias: bfloat16 [1024], P('shard'), may hold values from -3 to 3
- value_bias: bfloat16 [1024], P('shard'), may hold values from -3 to 3
- out_weight: bfloat16 [1024, 1024], P('shard'), may hold values from -0.75 to 0.75
- out_bias: bfloat16 [1024], P('shard'), may hold values from -3 to 3
- norm2_gain: bfloat16 [1024], P('shard'), may hold values from 0.099609375 to 1.8984375
- norm2_shift: bfloat16 [1024], P('shard'), may hold values from -3 to 3
- fc_weight: bfloat16 [1024, 4096], P('shard'), may hold values from -0.1875 to 0.1875
- fc_bias: bfloat16 [4096], P('shard'), may hold values from -3 to 3
- proj_weight: bfloat16 [4096, 1024], P('shard'), may hold values from -0.09375 to 0.09375
- proj_bias: bfloat16 [1024], P('shard'), may hold values from -3 to 3
Outputs:
- output: float32 [4096, 1024], P(('shard', 'replica'))
- tokens_grad: float32 [4096, 1024], P(('shard', 'replica'))
- norm1_gain_grad: float32 [1024], P('shard')
- norm1_shift_grad: float32 [1024], P('shard')
- qkv_weight_grad: float32 [1024, 3072], P('shard')
- query_bias_grad: float32 [1024], P('shard')
- value_bias_grad: float32 [1024], P('shard')
- out_weight_grad: float32 [1024, 1024], P('shard')
- out_bias_grad: float32 [1024], P('shard')
- norm2_gain_grad: float32 [1024], P('shard')
- norm2_shift_grad: float32 [1024], P('shard')
- fc_weight_grad: float32 [1024, 4096], P('shard')
- fc_bias_grad: float32 [4096], P('shard')
- proj_weight_grad: float32 [4096, 1024], P('shard')
- proj_bias_grad: float32 [1024], P('shard')
The draws below stay inside these ranges and needn't reach their ends.
Inputs may be any that keep to these rules, and one draw needn't show every extreme that they name: `segment_ids`: in each row (one device's tokens) the numbers never fall, every number from 0 to 3 occurs as one run of 1 to 64 positions, and one run holds exactly 64.
All inputs are finite; a program needn't handle non-finite values.
Results may differ from the reference program's by a relative error of at most 0.012.
Values may be sent and summed in bfloat16 or wider, within the bound.
A program may use at most 192 MiB of HBM per device.

```python
import math
import jax
import jax.numpy as jnp
import numpy as np
from jax import lax

D = 1024
HEADS = 16
HEAD = 64
FF = 4096
TOK_DEV = 128
SEGS = 4
MAXLEN = 64
TOKENS = 4096
DEVICES = 32


def block_levels(stream_key, shape, pieces, least, high):
    level = 1.0
    for dim, shards_of in pieces:
        heights = jax.random.uniform(jax.random.fold_in(jax.random.fold_in(stream_key, 6), dim), (shards_of,), jnp.float32, least / len(pieces), high / len(pieces))
        level = level * jnp.repeat(jnp.exp(heights), shape[dim] // shards_of).reshape((-1,) + (1,) * (len(shape) - 1 - dim))
    return level


def profile(number_of, total, most, lean):
    weights = [(1 << 20) // math.isqrt(rank ** lean) + 1 for rank in range(2, number_of + 1)]
    surplus, given = total - most - (number_of - 1), [1] * (number_of - 1)
    while surplus > 0:
        movable = [i for i in range(number_of - 1) if given[i] < most]
        mass, budget = sum([weights[i] for i in movable]), surplus
        for i in movable:
            more = min(most - given[i], max(1, budget * weights[i] // mass), surplus)
            given[i] = given[i] + more
            surplus = surplus - more
    return np.array([most] + given)


def ragged(rng, amount, total, most, skew):
    if amount == 2:
        one = jax.random.randint(rng, (), max(1, total - most), min(most, total - 1) + 1)
        return jnp.stack([one, total - one])
    tallies = jnp.asarray(profile(amount, total, most, skew), jnp.int32)
    pairs = (amount - 1) // 2
    source_of, taker = tallies[1:1 + 2 * pairs:2], tallies[2:2 + 2 * pairs:2]
    slack = jnp.minimum(source_of - 1, most - taker)
    passed = jax.random.randint(jax.random.fold_in(rng, 1), (pairs,), 0, 1 << 20) % (slack + 1)
    tallies = tallies.at[1:1 + 2 * pairs:2].set(source_of - passed).at[2:2 + 2 * pairs:2].set(taker + passed)
    return tallies[jax.random.permutation(jax.random.fold_in(rng, 2), amount)]


def noise(stream_key, extent, deviation, limit, shards=(), dtype=jnp.bfloat16):
    level = block_levels(stream_key, extent, shards, -0.22, 0.18) if shards else 1.0
    array = jax.random.normal(stream_key, extent, jnp.float32) * deviation * level
    return jnp.minimum(jnp.maximum(array, -limit), limit).astype(dtype)


def setup_inputs(seed: int = 0) -> dict:
    key_list = jax.random.split(jax.random.key(seed), 17)
    tokens = noise(key_list[0], (TOKENS, D), 1.0, 6.0, ((0, 32),), jnp.float32)
    segment_ids = jax.vmap(lambda own: jnp.searchsorted(jnp.cumsum(ragged(own, SEGS, TOK_DEV, MAXLEN, 2)), jnp.arange(TOK_DEV), side="right"))(jax.random.split(key_list[1], DEVICES)).reshape((DEVICES, TOK_DEV)).astype(jnp.int32)
    cotangent = noise(key_list[2], (TOKENS, D), 1.0, 6.0, ((0, 32),), jnp.float32)
    norm1_gain = jnp.clip(1.0 + 0.18 * jax.random.normal(key_list[3], (D,), jnp.float32), 0.099609375, 1.8984375).astype(jnp.bfloat16)
    norm1_shift = noise(key_list[4], (D,), 0.5, 3.0, ((0, 16),))
    qkv_weight = noise(key_list[5], (D, 3 * D), D ** -0.5, 0.1875, ((0, 16),))
    query_bias = noise(key_list[6], (D,), 0.5, 3.0, ((0, 16),))
    value_bias = noise(key_list[7], (D,), 0.5, 3.0, ((0, 16),))
    out_weight = noise(key_list[8], (D, D), (D // 16) ** -0.5, 0.75, ((0, 16),))
    out_bias = noise(key_list[9], (D,), 0.5, 3.0, ((0, 16),))
    norm2_gain = jnp.clip(1.0 + 0.18 * jax.random.normal(key_list[10], (D,), jnp.float32), 0.099609375, 1.8984375).astype(jnp.bfloat16)
    norm2_shift = noise(key_list[11], (D,), 0.5, 3.0, ((0, 16),))
    fc_weight = noise(key_list[12], (D, FF), D ** -0.5, 0.1875, ((0, 16),))
    fc_bias = noise(key_list[13], (FF,), 0.5, 3.0, ((0, 16),))
    proj_weight = noise(key_list[14], (FF, D), FF ** -0.5, 0.09375, ((0, 16),))
    proj_bias = noise(key_list[15], (D,), 0.5, 3.0, ((0, 16),))
    return dict(tokens=tokens, segment_ids=segment_ids, cotangent=cotangent, norm1_gain=norm1_gain, norm1_shift=norm1_shift, qkv_weight=qkv_weight, query_bias=query_bias, value_bias=value_bias, out_weight=out_weight, out_bias=out_bias, norm2_gain=norm2_gain, norm2_shift=norm2_shift, fc_weight=fc_weight, fc_bias=fc_bias, proj_weight=proj_weight, proj_bias=proj_bias)


EPS = 1e-05
GELU_C = 0.7978845608028654
GELU_A = 0.044715

def layer_norm(values, gain, shift):
    row_mean = lax.optimization_barrier(jnp.mean(values, axis=-1, keepdims=True))
    centered = values - row_mean
    inv_std = lax.rsqrt(lax.optimization_barrier(jnp.mean(centered * centered, axis=-1, keepdims=True)) + EPS)
    normed = centered * inv_std
    return (normed * gain.astype(jnp.float32) + shift.astype(jnp.float32), normed, inv_std)

def norm_back(grad_out, normed, inv_std, gain):
    scaled = grad_out * gain.astype(jnp.float32)
    return inv_std * (scaled - lax.optimization_barrier(jnp.mean(scaled, axis=-1, keepdims=True)) - normed * lax.optimization_barrier(jnp.mean(scaled * normed, axis=-1, keepdims=True)))

def gelu_pair(pre_act):
    tangent = jnp.tanh(GELU_C * (pre_act + GELU_A * pre_act * pre_act * pre_act))
    value = 0.5 * pre_act * (1.0 + tangent)
    slope = 0.5 * (1.0 + tangent) + 0.5 * pre_act * (1.0 - tangent * tangent) * GELU_C * (1.0 + 3.0 * GELU_A * pre_act * pre_act)
    return (value, slope)

def block(tokens, segment_row, cotangent, params):
    norm1_gain, norm1_shift, qkv_weight, query_bias, value_bias, out_weight, out_bias, norm2_gain, norm2_shift, fc_weight, fc_bias, proj_weight, proj_bias = params
    rows = tokens.shape[0]
    width = tokens.shape[1]
    scale = HEAD ** (-0.5)
    ln1, normed1, inv1 = layer_norm(tokens, norm1_gain, norm1_shift)
    input1 = ln1.astype(jnp.bfloat16)
    qkv_bias = jnp.concatenate([query_bias.astype(jnp.float32), jnp.zeros((width,), jnp.float32), value_bias.astype(jnp.float32)])
    projected = jnp.dot(input1, qkv_weight, preferred_element_type=jnp.float32) + qkv_bias
    query = projected[:, :width].reshape(rows, HEADS, HEAD).astype(jnp.bfloat16)
    keyed = projected[:, width:2 * width].reshape(rows, HEADS, HEAD).astype(jnp.bfloat16)
    valued = projected[:, 2 * width:].reshape(rows, HEADS, HEAD).astype(jnp.bfloat16)
    scores = jnp.einsum('qhd,khd->hqk', query.astype(jnp.float32), keyed.astype(jnp.float32)) * scale
    position = jnp.arange(rows)
    allowed = (segment_row[:, None] == segment_row[None, :]) & (position[None, :] <= position[:, None])
    scores = jnp.where(allowed[None], scores, -1e+30)
    top = lax.optimization_barrier(jnp.max(scores, axis=-1, keepdims=True))
    log_total = top + jnp.log(lax.optimization_barrier(jnp.sum(jnp.exp(scores - top), axis=-1, keepdims=True)))
    probs = jnp.exp(scores - log_total)
    probs_low = probs.astype(jnp.bfloat16)
    context = jnp.einsum('hqk,khd->qhd', probs_low.astype(jnp.float32), valued.astype(jnp.float32))
    context = context.reshape(rows, width).astype(jnp.bfloat16)
    middle = tokens + jnp.dot(context, out_weight, preferred_element_type=jnp.float32) + out_bias.astype(jnp.float32)
    ln2, normed2, inv2 = layer_norm(middle, norm2_gain, norm2_shift)
    input2 = ln2.astype(jnp.bfloat16)
    pre_act = jnp.dot(input2, fc_weight, preferred_element_type=jnp.float32) + fc_bias.astype(jnp.float32)
    gelu_value, gelu_slope = gelu_pair(pre_act)
    activated = gelu_value.astype(jnp.bfloat16)
    output = middle + jnp.dot(activated, proj_weight, preferred_element_type=jnp.float32) + proj_bias.astype(jnp.float32)
    grad_proj_bias = lax.optimization_barrier(jnp.sum(cotangent, axis=0))
    cot_low = cotangent.astype(jnp.bfloat16)
    grad_proj_weight = jnp.dot(activated.T, cot_low, preferred_element_type=jnp.float32)
    grad_pre = jnp.dot(cot_low, proj_weight.T, preferred_element_type=jnp.float32) * gelu_slope
    grad_fc_bias = lax.optimization_barrier(jnp.sum(grad_pre, axis=0))
    grad_pre_low = grad_pre.astype(jnp.bfloat16)
    grad_fc_weight = jnp.dot(input2.T, grad_pre_low, preferred_element_type=jnp.float32)
    grad_in2 = jnp.dot(grad_pre_low, fc_weight.T, preferred_element_type=jnp.float32)
    grad_gain2 = lax.optimization_barrier(jnp.sum(grad_in2 * normed2, axis=0))
    grad_shift2 = lax.optimization_barrier(jnp.sum(grad_in2, axis=0))
    grad_middle = cotangent + norm_back(grad_in2, normed2, inv2, norm2_gain)
    grad_out_bias = lax.optimization_barrier(jnp.sum(grad_middle, axis=0))
    mid_low = grad_middle.astype(jnp.bfloat16)
    grad_out_weight = jnp.dot(context.T, mid_low, preferred_element_type=jnp.float32)
    grad_context = jnp.dot(mid_low, out_weight.T, preferred_element_type=jnp.float32)
    grad_context = grad_context.reshape(rows, HEADS, HEAD).astype(jnp.bfloat16)
    grad_value = jnp.einsum('hqk,qhd->khd', probs_low.astype(jnp.float32), grad_context.astype(jnp.float32))
    grad_probs = jnp.einsum('qhd,khd->hqk', grad_context.astype(jnp.float32), valued.astype(jnp.float32))
    grad_scores = probs * (grad_probs - lax.optimization_barrier(jnp.sum(probs * grad_probs, axis=-1, keepdims=True))) * scale
    grad_scores = grad_scores.astype(jnp.bfloat16)
    grad_query = jnp.einsum('hqk,khd->qhd', grad_scores.astype(jnp.float32), keyed.astype(jnp.float32))
    grad_key = jnp.einsum('hqk,qhd->khd', grad_scores.astype(jnp.float32), query.astype(jnp.float32))
    grad_query = grad_query.reshape(rows, width)
    grad_key = grad_key.reshape(rows, width)
    grad_value = grad_value.reshape(rows, width)
    grad_query_bias = lax.optimization_barrier(jnp.sum(grad_query, axis=0))
    grad_value_bias = lax.optimization_barrier(jnp.sum(grad_value, axis=0))
    grad_qkv = jnp.concatenate([grad_query, grad_key, grad_value], axis=1).astype(jnp.bfloat16)
    grad_qkv_weight = jnp.dot(input1.T, grad_qkv, preferred_element_type=jnp.float32)
    grad_in1 = jnp.dot(grad_qkv, qkv_weight.T, preferred_element_type=jnp.float32)
    grad_gain1 = lax.optimization_barrier(jnp.sum(grad_in1 * normed1, axis=0))
    grad_shift1 = lax.optimization_barrier(jnp.sum(grad_in1, axis=0))
    tokens_grad = grad_middle + norm_back(grad_in1, normed1, inv1, norm1_gain)
    grads = (grad_gain1, grad_shift1, grad_qkv_weight, grad_query_bias, grad_value_bias, grad_out_weight, grad_out_bias, grad_gain2, grad_shift2, grad_fc_weight, grad_fc_bias, grad_proj_weight, grad_proj_bias)
    return (output, tokens_grad, grads)

def reference(tokens, segment_ids, cotangent, norm1_gain, norm1_shift, qkv_weight, query_bias, value_bias, out_weight, out_bias, norm2_gain, norm2_shift, fc_weight, fc_bias, proj_weight, proj_bias):
    params = (norm1_gain, norm1_shift, qkv_weight, query_bias, value_bias, out_weight, out_bias, norm2_gain, norm2_shift, fc_weight, fc_bias, proj_weight, proj_bias)
    blocks_in = tokens.reshape(-1, TOK_DEV, D)
    blocks_cot = cotangent.reshape(-1, TOK_DEV, D)
    zero_grads = tuple((jnp.zeros(item.shape, jnp.float32) for item in params))

    def one_block(carry, inputs):
        output, tokens_grad, grads = block(inputs[0], inputs[1], inputs[2], params)
        return (tuple((left + right for left, right in zip(carry, grads))), (output, tokens_grad))
    grads, (outputs, token_grads) = lax.scan(one_block, zero_grads, (blocks_in, segment_ids, blocks_cot))
    return (outputs.reshape(-1, D), token_grads.reshape(-1, D), grads[0], grads[1], grads[2], grads[3], grads[4], grads[5], grads[6], grads[7], grads[8], grads[9], grads[10], grads[11], grads[12])
```

```python
import jax
import jax.numpy as jnp
from jax import lax
from jax.sharding import Mesh
from jax.sharding import PartitionSpec as P

HEADS = 16
HEAD = 64


EPS = 1e-05
GELU_C = 0.7978845608028654
GELU_A = 0.044715

GB = 4
GV = 2
B_AXES = ("bh", "bl")
G_AXES = ("bh", "bl", "v")
S_AXES = ("a", "bh", "bl")
ALL_AXES = ("a", "bh", "bl", "u", "v")
F32 = jnp.float32
BF16 = jnp.bfloat16


def layer_norm(values, gain, shift):
    row_mean = jnp.mean(values, axis=-1, keepdims=True)
    centered = values - row_mean
    inv_std = lax.rsqrt(jnp.mean(centered * centered, axis=-1, keepdims=True) + EPS)
    normed = centered * inv_std
    return (normed * gain + shift, normed, inv_std)


def norm_back(grad_out, normed, inv_std, gain):
    scaled = grad_out * gain
    return inv_std * (
        scaled
        - jnp.mean(scaled, axis=-1, keepdims=True)
        - normed * jnp.mean(scaled * normed, axis=-1, keepdims=True)
    )


def gelu_pair(pre_act):
    tangent = jnp.tanh(GELU_C * (pre_act + GELU_A * pre_act * pre_act * pre_act))
    value = 0.5 * pre_act * (1.0 + tangent)
    slope = 0.5 * (1.0 + tangent) + 0.5 * pre_act * (1.0 - tangent * tangent) * GELU_C * (
        1.0 + 3.0 * GELU_A * pre_act * pre_act
    )
    return (value, slope)


def contract(left, right, left_axis, right_axis):
    return lax.dot_general(
        left, right, (((left_axis,), (right_axis,)), ((), ())), preferred_element_type=F32
    )


def pick(values, index, axis):
    return lax.dynamic_index_in_dim(values, index, axis, keepdims=False)


def gather_group(values):
    return lax.all_gather(values, G_AXES, axis=0, tiled=True)


def scatter_group(values):
    return lax.psum_scatter(
        values.astype(BF16), G_AXES, scatter_dimension=0, tiled=True
    ).astype(F32)


def on_device(
    tokens,
    segment_ids,
    cotangent,
    norm1_gain,
    norm1_shift,
    qkv_weight,
    query_bias,
    value_bias,
    out_weight,
    out_bias,
    norm2_gain,
    norm2_shift,
    fc_weight,
    fc_bias,
    proj_weight,
    proj_bias,
):
    rows, width = tokens.shape
    n_a = lax.axis_size("a")
    n_bl = lax.axis_size("bl")
    n_bh = lax.axis_size("bh")
    n_u = lax.axis_size("u")
    shards = n_a * GB
    depth = width // shards
    hidden_rows = fc_bias.shape[0]
    hidden = hidden_rows * shards
    half = hidden_rows // GV
    my_hidden = n_a * half
    heads_here = HEADS // (GB * GV)
    cols = heads_here * HEAD
    scale = HEAD ** (-0.5)
    v = lax.axis_index("v")
    bl = lax.axis_index("bl")
    bh = lax.axis_index("bh")
    b = bh * n_bl + bl
    me = lax.axis_index("a") * GB + b

    small = jnp.concatenate(
        [
            norm1_gain,
            norm1_shift,
            query_bias,
            value_bias,
            out_bias,
            norm2_gain,
            norm2_shift,
            proj_bias,
            fc_bias,
        ]
    )
    small = lax.all_gather(small, S_AXES, axis=0).astype(F32)
    gain1, shift1, bias_query, bias_value, bias_out, gain2, shift2, bias_proj = (
        small[:, i * depth : (i + 1) * depth].reshape(width) for i in range(8)
    )
    bias_fc = small[:, 8 * depth :]

    def head_split(values):
        lead = values.shape[:-1]
        n = len(lead)
        values = values.reshape(*lead, n_bl, GV, heads_here, n_bh, HEAD)
        order = (n + 3, n, n + 1, *range(n), n + 2, n + 4)
        return values.transpose(order).reshape(n_bh, n_bl, GV, *lead, cols)

    qkv = pick(head_split(qkv_weight.reshape(depth, 3, width)), v, 2)
    qkv = qkv.reshape(GB, depth, 3 * cols)
    fc = pick(fc_weight.reshape(depth, n_a, GB, GV, half), v, 3)
    fc = fc.transpose(2, 0, 1, 3).reshape(GB, depth, my_hidden)
    qkv = lax.all_to_all(qkv, B_AXES, 0, 0, tiled=True).reshape(GB * depth, 3 * cols)
    fc = lax.all_to_all(fc, B_AXES, 0, 0, tiled=True).reshape(GB * depth, my_hidden)
    w_qkv = lax.all_gather(qkv, "a", axis=0, tiled=True)
    w_out = lax.all_gather(out_weight, ("a", "bl"), axis=0, tiled=True)
    slot = bl * GV + v
    w_out = lax.dynamic_slice_in_dim(w_out, slot * cols, cols, 0)
    w_fc = lax.all_gather(fc, "a", axis=0, tiled=True)
    w_proj = lax.all_gather(
        lax.dynamic_slice_in_dim(proj_weight, v * half, half, 0), "a", axis=0, tiled=True
    )

    def my_heads(values):
        return pick(head_split(values).reshape(GB, GV, cols), b, 0)

    bq = pick(my_heads(bias_query), v, 0)
    bv = pick(my_heads(bias_value), v, 0)
    b_fc = pick(pick(bias_fc.reshape(n_a, GB, GV, half), b, 1), v, 1).reshape(my_hidden)

    cot_low = gather_group(cotangent.astype(BF16))
    segments = lax.all_gather(segment_ids[0], G_AXES, axis=0)

    ln1, normed1, inv1 = layer_norm(tokens, gain1, shift1)
    input1 = gather_group(ln1.astype(BF16))
    blocks = GB * GV
    qkv_bias = jnp.concatenate([bq, jnp.zeros((cols,), F32), bv])
    projected = jnp.dot(input1, w_qkv, preferred_element_type=F32) + qkv_bias
    projected = projected.astype(BF16).reshape(blocks, rows, 3, heads_here, HEAD)
    query, keyed, valued = projected[:, :, 0], projected[:, :, 1], projected[:, :, 2]
    scores = jnp.einsum("nqhd,nkhd->nhqk", query, keyed, preferred_element_type=F32) * scale
    position = jnp.arange(rows)
    allowed = (segments[:, :, None] == segments[:, None, :]) & (
        position[None, :] <= position[:, None]
    )
    scores = jnp.where(allowed[:, None], scores, -1e30)
    top = jnp.max(scores, axis=-1, keepdims=True)
    log_total = top + jnp.log(jnp.sum(jnp.exp(scores - top), axis=-1, keepdims=True))
    probs = jnp.exp(scores - log_total)
    probs_low = probs.astype(BF16)
    context = jnp.einsum("nhqk,nkhd->nqhd", probs_low, valued, preferred_element_type=F32)
    context = context.reshape(blocks * rows, cols).astype(BF16)
    middle = (
        tokens + scatter_group(jnp.dot(context, w_out, preferred_element_type=F32)) + bias_out
    )

    ln2, normed2, inv2 = layer_norm(middle, gain2, shift2)
    input2 = gather_group(ln2.astype(BF16))
    pre_act = jnp.dot(input2, w_fc, preferred_element_type=F32) + b_fc
    gelu_value, gelu_slope = gelu_pair(pre_act)
    activated = gelu_value.astype(BF16)
    grad_pre = contract(cot_low, w_proj, 1, 1) * gelu_slope
    grad_pre_low = grad_pre.astype(BF16)
    grad_in2 = scatter_group(contract(grad_pre_low, w_fc, 1, 1))
    output = (
        middle + scatter_group(jnp.dot(activated, w_proj, preferred_element_type=F32)) + bias_proj
    )
    grad_fc_bias = jnp.sum(grad_pre, axis=0)
    grad_proj_weight = contract(activated, cot_low, 0, 0)
    grad_fc_weight = contract(input2, grad_pre_low, 0, 0)

    def reduce_a(values, axes="a"):
        values = lax.psum_scatter(values.astype(BF16), axes, scatter_dimension=0, tiled=True)
        return lax.psum(values, "u") if n_u > 1 else values

    share_proj = lax.all_gather(reduce_a(grad_proj_weight), "v", axis=0, tiled=True).astype(F32)

    def columns_home(values):
        values = reduce_a(values).reshape(GB, depth, values.shape[1])
        values = lax.all_to_all(values, B_AXES, 0, 0, tiled=True)
        return lax.all_gather(values, "v", axis=0)

    share_fc = columns_home(grad_fc_weight).reshape(GV, GB, depth, n_a, half)
    share_fc = share_fc.transpose(2, 3, 1, 0, 4).reshape(depth, hidden).astype(F32)

    grad_gain2 = jnp.sum(grad_in2 * normed2, axis=0)
    grad_shift2 = jnp.sum(grad_in2, axis=0)
    grad_middle = cotangent + norm_back(grad_in2, normed2, inv2, gain2)

    mid_low = gather_group(grad_middle.astype(BF16))
    grad_out_weight = contract(context, mid_low, 0, 0)
    grad_context = contract(mid_low, w_out, 1, 1)
    grad_context = grad_context.astype(BF16).reshape(blocks, rows, heads_here, HEAD)
    grad_value = jnp.einsum("nhqk,nqhd->nkhd", probs_low, grad_context, preferred_element_type=F32)
    grad_probs = jnp.einsum("nqhd,nkhd->nhqk", grad_context, valued, preferred_element_type=F32)
    grad_scores = probs * (grad_probs - jnp.sum(probs * grad_probs, axis=-1, keepdims=True)) * scale
    grad_scores = grad_scores.astype(BF16)
    grad_query = jnp.einsum("nhqk,nkhd->nqhd", grad_scores, keyed, preferred_element_type=F32)
    grad_key = jnp.einsum("nhqk,nqhd->nkhd", grad_scores, query, preferred_element_type=F32)
    grad_query, grad_key, grad_value = (
        g.reshape(blocks * rows, cols) for g in (grad_query, grad_key, grad_value)
    )
    grad_query_bias = jnp.sum(grad_query, axis=0)
    grad_value_bias = jnp.sum(grad_value, axis=0)
    grad_qkv = jnp.concatenate([grad_query, grad_key, grad_value], axis=1).astype(BF16)
    grad_in1 = scatter_group(contract(grad_qkv, w_qkv, 1, 1))
    grad_qkv_weight = contract(input1, grad_qkv, 0, 0)

    share_qkv = columns_home(grad_qkv_weight).reshape(
        GV, n_bh, n_bl, depth, 3, heads_here, HEAD
    )
    share_qkv = share_qkv.transpose(3, 4, 2, 0, 5, 1, 6).reshape(depth, 3 * width).astype(F32)

    out_full = jnp.zeros((depth * n_a * n_bl, width), BF16)
    out_full = lax.dynamic_update_slice_in_dim(
        out_full, grad_out_weight.astype(BF16), slot * cols, 0
    )
    share_out = lax.psum(reduce_a(out_full, ("a", "bl")), "v").astype(F32)

    grad_gain1 = jnp.sum(grad_in1 * normed1, axis=0)
    grad_shift1 = jnp.sum(grad_in1, axis=0)
    tokens_grad = grad_middle + norm_back(grad_in1, normed1, inv1, gain1)

    def heads_full(values):
        here = (jnp.arange(GB * GV) == b * GV + v).astype(F32)
        values = here[:, None] * values[None, :]
        values = values.reshape(n_bh, n_bl, GV, heads_here, HEAD).transpose(1, 2, 3, 0, 4)
        return values.reshape(width)

    here = (jnp.arange(GB * GV) == b * GV + v).astype(F32)
    fc_full = here.reshape(1, GB, GV, 1) * grad_fc_bias.reshape(n_a, 1, 1, half)
    sums = [
        jnp.sum(cotangent, axis=0),
        grad_gain2,
        grad_shift2,
        jnp.sum(grad_middle, axis=0),
        heads_full(grad_query_bias),
        heads_full(grad_value_bias),
        grad_gain1,
        grad_shift1,
    ]
    sums = [s.reshape(shards, depth) for s in sums]
    sums = jnp.concatenate([*sums, fc_full.reshape(shards, hidden_rows)], axis=1)
    sums = pick(lax.psum(sums, ALL_AXES), me, 0)
    (
        share_proj_bias,
        share_gain2,
        share_shift2,
        share_out_bias,
        share_query_bias,
        share_value_bias,
        share_gain1,
        share_shift1,
    ) = (sums[i * depth : (i + 1) * depth] for i in range(8))
    share_fc_bias = sums[8 * depth :]
    return (
        output,
        tokens_grad,
        share_gain1,
        share_shift1,
        share_qkv,
        share_query_bias,
        share_value_bias,
        share_out,
        share_out_bias,
        share_gain2,
        share_shift2,
        share_fc,
        share_fc_bias,
        share_proj,
        share_proj_bias,
    )


def solution(mesh):
    shard, replica = mesh.shape["shard"], mesh.shape["replica"]
    head_parts = max(1, HEAD * shard // (HEADS * HEAD))
    grid = mesh.devices.reshape(
        shard // GB, GB // head_parts, head_parts, replica // GV, GV
    )
    inner = Mesh(grid, ALL_AXES)
    row = P(ALL_AXES, None)
    vec = P(S_AXES)
    mat = P(S_AXES, None)
    in_specs = (
        row, row, row, vec, vec, mat, vec, vec, mat, vec, vec, vec, mat, vec, mat, vec,
    )
    out_specs = (
        row, row, vec, vec, mat, vec, vec, mat, vec, vec, vec, mat, vec, mat, vec,
    )
    return jax.shard_map(
        on_device, mesh=inner, in_specs=in_specs, out_specs=out_specs, check_vma=False
    )
```

```python
import functools

import jax
import jax.numpy as jnp
from jax import lax
from jax.experimental import pallas as pl
from jax.experimental.pallas import tpu as pltpu
from jax.sharding import Mesh
from jax.sharding import PartitionSpec as P

HEADS = 16
HEAD = 64


EPS = 1e-05
GELU_C = 0.7978845608028654
GELU_A = 0.044715

GB = 4
GV = 2
G = GB * GV
B_AXES = ("b1", "b0")
G_AXES = ("b1", "b0", "v")
S_AXES = ("a", "b1", "b0")
ALL_AXES = ("a", "b1", "b0", "u", "v")
MESH = pl.DeviceIdType.MESH
VMEM = pl.BlockSpec(memory_space=pltpu.VMEM)
F32 = jnp.float32
BF16 = jnp.bfloat16


def layer_norm(values, gain, shift):
    row_mean = jnp.mean(values, axis=-1, keepdims=True)
    centered = values - row_mean
    inv_std = lax.rsqrt(jnp.mean(centered * centered, axis=-1, keepdims=True) + EPS)
    normed = centered * inv_std
    return (normed * gain + shift, normed, inv_std)


def norm_back(grad_out, normed, inv_std, gain):
    scaled = grad_out * gain
    return inv_std * (
        scaled
        - jnp.mean(scaled, axis=-1, keepdims=True)
        - normed * jnp.mean(scaled * normed, axis=-1, keepdims=True)
    )


def gelu_pair(pre_act):
    tangent = jnp.tanh(GELU_C * (pre_act + GELU_A * pre_act * pre_act * pre_act))
    value = 0.5 * pre_act * (1.0 + tangent)
    slope = 0.5 * (1.0 + tangent) + 0.5 * pre_act * (1.0 - tangent * tangent) * GELU_C * (
        1.0 + 3.0 * GELU_A * pre_act * pre_act
    )
    return (value, slope)


def contract(left, right, left_axis, right_axis):
    return lax.dot_general(
        left, right, (((left_axis,), (right_axis,)), ((), ())), preferred_element_type=F32
    )


def pick(values, index, axis):
    return lax.dynamic_index_in_dim(values, index, axis, keepdims=False)


def gather_group(values):
    return lax.all_gather(values, G_AXES, axis=0, tiled=True)


def scatter_group(values):
    return lax.psum_scatter(
        values.astype(BF16), G_AXES, scatter_dimension=0, tiled=True
    ).astype(F32)


def meet(peers):
    barrier = pltpu.get_barrier_semaphore()
    for peer in peers:
        pl.semaphore_signal(barrier, inc=1, device_id=peer, device_id_type=MESH)
    pl.semaphore_wait(barrier, len(peers))


def remote(src, dst, send, recv, peer):
    return pltpu.make_async_remote_copy(
        src_ref=src, dst_ref=dst, send_sem=send, recv_sem=recv, device_id=peer, device_id_type=MESH
    )


def group_place():
    b1, b0, v = (lax.axis_index(axis) for axis in G_AXES)
    chips = [((b1 + (d >> 1)) % 2, (v + (d & 1)) % 2) for d in range(4)]
    peers = [{"b1": c1, "b0": b0, "v": cv} for c1, cv in chips]
    partner = {"b1": b1, "b0": 1 - b0, "v": v}
    return b0, chips, peers, partner


def member(c1, b0, cv):
    return (c1 * 2 + b0) * GV + cv


def gather_kernel(x_ref, out_ref, send, recv, pass_send, pass_recv):
    b0, chips, peers, partner = group_place()
    mine = [member(c1, b0, cv) for c1, cv in chips]
    meet([partner, *peers[1:]])
    first = {}
    for d in (3, 1, 2, 0):
        first[d] = remote(
            x_ref, out_ref.at[mine[0]], send.at[d], recv.at[d], peers[d] if d else partner
        )
        first[d].start()
    out_ref[mine[0]] = x_ref[...]
    passed = []
    for d in (1, 2, 3):
        first[d].wait_recv()
        block = out_ref.at[mine[d]]
        copy = remote(block, block, pass_send.at[d - 1], pass_recv.at[d - 1], partner)
        copy.start()
        passed.append(copy)
    first[0].wait_recv()
    for copy in first.values():
        copy.wait_send()
    for copy in passed:
        copy.wait()


def scatter_kernel(
    y_ref, out_ref, came, total, arrived, send, recv, chip_send, chip_recv
):
    b0, chips, peers, partner = group_place()
    meet([partner, *peers[1:]])
    pair = {}
    for d in (3, 1, 2, 0):
        pair[d] = remote(
            y_ref.at[member(chips[d][0], 1 - b0, chips[d][1])],
            came.at[d],
            send.at[d],
            recv.at[d],
            partner,
        )
        pair[d].start()
    sent = {}
    for d in (3, 1, 2):
        pair[d].wait_recv()
        own = y_ref[member(chips[d][0], b0, chips[d][1])].astype(F32)
        total[d - 1] = (own + came[d].astype(F32)).astype(BF16)
        sent[d] = remote(
            total.at[d - 1], arrived.at[d - 1], chip_send.at[d - 1], chip_recv.at[d - 1], peers[d]
        )
        sent[d].start()
    pair[0].wait_recv()
    out_ref[...] = y_ref[member(chips[0][0], b0, chips[0][1])].astype(F32) + came[0].astype(F32)
    for d in (1, 2, 3):
        sent[d].wait_recv()
        out_ref[...] += arrived[d - 1].astype(F32)
    for d in range(4):
        pair[d].wait_send()
    for d in (1, 2, 3):
        sent[d].wait_send()


def call(kernel, out_shape, scratch, collective_id, cost, *args):
    many = isinstance(out_shape, tuple)
    return pl.pallas_call(
        kernel,
        out_shape=out_shape,
        in_specs=[VMEM] * len(args),
        out_specs=(VMEM,) * len(out_shape) if many else VMEM,
        scratch_shapes=scratch,
        cost_estimate=pl.CostEstimate(flops=0, bytes_accessed=cost, transcendentals=0),
        compiler_params=pltpu.CompilerParams(
            collective_id=collective_id, has_side_effects=True, vmem_limit_bytes=24 << 20
        ),
    )(*args)


def dma(n):
    return pltpu.SemaphoreType.DMA((n,))


def gather_now(values):
    rows, width = values.shape
    out = jax.ShapeDtypeStruct((G, rows, width), values.dtype)
    scratch = [dma(4), dma(4), dma(3), dma(3)]
    return call(gather_kernel, out, scratch, 0, 32 << 20, values).reshape(G * rows, width)


def scatter_now(values):
    rows, width = values.shape[0] // G, values.shape[1]
    block = (rows, width)
    scratch = [
        pltpu.VMEM((4, *block), BF16),
        pltpu.VMEM((3, *block), BF16),
        pltpu.VMEM((3, *block), BF16),
        dma(4),
        dma(4),
        dma(3),
        dma(3),
    ]
    out = jax.ShapeDtypeStruct(block, F32)
    return call(
        scatter_kernel, out, scratch, 1, 32 << 20, values.astype(BF16).reshape(G, *block)
    )


def shard_peers(shards):
    me = (lax.axis_index("a") * 2 + lax.axis_index("b1")) * 2 + lax.axis_index("b0")
    flats = [(me + k) % shards for k in range(shards)]
    peers = [{"a": f // GB, "b1": (f // 2) % 2, "b0": f % 2} for f in flats]
    return flats, peers


def start_kernel(shards, p_ref, s_ref, all_ref, seg_ref, send, recv, seg_send, seg_recv):
    flats, peers = shard_peers(shards)
    b1, b0, v = (lax.axis_index(axis) for axis in G_AXES)
    me = member(b1, b0, v)
    others = [(me + k) % G for k in range(G)]
    group = [{"b1": o // 4, "b0": (o // 2) % 2, "v": o % 2} for o in others]
    meet([*peers[1:], *group[1:]])
    copies = []
    for k in range(1, shards):
        copies.append(remote(p_ref, all_ref.at[flats[0]], send.at[k], recv.at[k], peers[k]))
        copies[-1].start()
    for k in range(1, G):
        copies.append(remote(s_ref, seg_ref.at[me], seg_send.at[k], seg_recv.at[k], group[k]))
        copies[-1].start()
    all_ref[flats[0]] = p_ref[...]
    seg_ref[me] = s_ref[...]
    for copy in copies:
        copy.wait()


def start_now(small, segments, shards):
    small = small.astype(F32).reshape(-1, 128)
    segments = segments.astype(F32)
    out = (
        jax.ShapeDtypeStruct((shards, *small.shape), F32),
        jax.ShapeDtypeStruct((G, *segments.shape), F32),
    )
    scratch = [dma(shards), dma(shards), dma(G), dma(G)]
    kernel = functools.partial(start_kernel, shards)
    params, segs = call(kernel, out, scratch, 2, 8 << 20, small, segments)
    return params.reshape(shards, -1), segs[:, 0]


def sums_kernel(shards, n_u, x_ref, out_ref, came, total, extra, send, recv, r_send, r_recv):
    flats, peers = shard_peers(shards)
    u, v = lax.axis_index("u"), lax.axis_index("v")
    copies_n = n_u * GV
    place = u * GV + v
    twins = [(place + k) % copies_n for k in range(copies_n)]
    twins = [{"u": t // GV, "v": t % GV} for t in twins]
    meet([*peers[1:], *twins[1:]])
    copies = []
    for k in range(1, shards):
        copies.append(
            remote(x_ref.at[flats[k]], came.at[k], send.at[k], recv.at[k], peers[k])
        )
        copies[-1].start()
    value = x_ref[flats[0]]
    for k, copy in enumerate(copies, 1):
        copy.wait_recv()
        value += came[k]
    total[...] = value
    again = []
    for k in range(1, copies_n):
        again.append(remote(total, extra.at[k], r_send.at[k], r_recv.at[k], twins[k]))
        again[-1].start()
    for k, copy in enumerate(again, 1):
        copy.wait_recv()
        value += extra[k]
    out_ref[...] = value
    for copy in [*copies, *again]:
        copy.wait_send()


def sums_now(values, n_u):
    shards, n = values.shape
    values = values.reshape(shards, n // 128, 128)
    block = values.shape[1:]
    scratch = [
        pltpu.VMEM((shards, *block), F32),
        pltpu.VMEM(block, F32),
        pltpu.VMEM((n_u * GV, *block), F32),
        dma(shards),
        dma(shards),
        dma(n_u * GV),
        dma(n_u * GV),
    ]
    out = jax.ShapeDtypeStruct(block, F32)
    kernel = functools.partial(sums_kernel, shards, n_u)
    return call(kernel, out, scratch, 3, 8 << 20, values).reshape(n)


def on_device(
    tokens,
    segment_ids,
    cotangent,
    norm1_gain,
    norm1_shift,
    qkv_weight,
    query_bias,
    value_bias,
    out_weight,
    out_bias,
    norm2_gain,
    norm2_shift,
    fc_weight,
    fc_bias,
    proj_weight,
    proj_bias,
):
    rows, width = tokens.shape
    n_a = lax.axis_size("a")
    n_u = lax.axis_size("u")
    shards = n_a * GB
    depth = width // shards
    n_bl = max(1, HEAD // depth)
    n_bh = GB // n_bl
    row_axes = ("a",) if n_bl == 1 else ("a", "b0")
    hidden_rows = fc_bias.shape[0]
    hidden = hidden_rows * shards
    half = hidden_rows // GV
    my_hidden = n_a * half
    heads_here = HEADS // (GB * GV)
    cols = heads_here * HEAD
    scale = HEAD ** (-0.5)
    v = lax.axis_index("v")
    b = lax.axis_index("b1") * 2 + lax.axis_index("b0")
    bl = b % n_bl

    small = jnp.concatenate(
        [
            norm1_gain,
            norm1_shift,
            query_bias,
            value_bias,
            out_bias,
            norm2_gain,
            norm2_shift,
            proj_bias,
            fc_bias,
        ]
    )
    small, segments = start_now(small, segment_ids, shards)
    gain1, shift1, bias_query, bias_value, bias_out, gain2, shift2, bias_proj = (
        small[:, i * depth : (i + 1) * depth].reshape(width) for i in range(8)
    )
    bias_fc = small[:, 8 * depth :]

    def head_split(values):
        lead = values.shape[:-1]
        n = len(lead)
        values = values.reshape(*lead, n_bl, GV, heads_here, n_bh, HEAD)
        order = (n + 3, n, n + 1, *range(n), n + 2, n + 4)
        return values.transpose(order).reshape(n_bh, n_bl, GV, *lead, cols)

    qkv = pick(head_split(qkv_weight.reshape(depth, 3, width)), v, 2)
    qkv = qkv.reshape(GB, depth, 3 * cols)
    fc = pick(fc_weight.reshape(depth, n_a, GB, GV, half), v, 3)
    fc = fc.transpose(2, 0, 1, 3).reshape(GB, depth, my_hidden)
    qkv = lax.all_to_all(qkv, B_AXES, 0, 0, tiled=True).reshape(GB * depth, 3 * cols)
    fc = lax.all_to_all(fc, B_AXES, 0, 0, tiled=True).reshape(GB * depth, my_hidden)
    w_qkv = lax.all_gather(qkv, "a", axis=0, tiled=True)
    w_out = lax.all_gather(out_weight, row_axes, axis=0, tiled=True)
    slot = bl * GV + v
    w_out = lax.dynamic_slice_in_dim(w_out, slot * cols, cols, 0)
    w_fc = lax.all_gather(fc, "a", axis=0, tiled=True)
    w_proj = lax.all_gather(
        lax.dynamic_slice_in_dim(proj_weight, v * half, half, 0), "a", axis=0, tiled=True
    )

    def my_heads(values):
        return pick(head_split(values).reshape(GB, GV, cols), b, 0)

    bq = pick(my_heads(bias_query), v, 0)
    bv = pick(my_heads(bias_value), v, 0)
    b_fc = pick(pick(bias_fc.reshape(n_a, GB, GV, half), b, 1), v, 1).reshape(my_hidden)

    cot_low = gather_group(cotangent.astype(BF16))

    ln1, normed1, inv1 = layer_norm(tokens, gain1, shift1)
    input1 = gather_now(ln1.astype(BF16))
    blocks = GB * GV
    qkv_bias = jnp.concatenate([bq, jnp.zeros((cols,), F32), bv])
    projected = jnp.dot(input1, w_qkv, preferred_element_type=F32) + qkv_bias
    projected = projected.astype(BF16).reshape(blocks, rows, 3, heads_here, HEAD)
    query, keyed, valued = projected[:, :, 0], projected[:, :, 1], projected[:, :, 2]
    scores = jnp.einsum("nqhd,nkhd->nhqk", query, keyed, preferred_element_type=F32) * scale
    position = jnp.arange(rows)
    allowed = (segments[:, :, None] == segments[:, None, :]) & (
        position[None, :] <= position[:, None]
    )
    scores = jnp.where(allowed[:, None], scores, -1e30)
    top = jnp.max(scores, axis=-1, keepdims=True)
    log_total = top + jnp.log(jnp.sum(jnp.exp(scores - top), axis=-1, keepdims=True))
    probs = jnp.exp(scores - log_total)
    probs_low = probs.astype(BF16)
    context = jnp.einsum("nhqk,nkhd->nqhd", probs_low, valued, preferred_element_type=F32)
    context = context.reshape(blocks * rows, cols).astype(BF16)
    middle = (
        tokens + scatter_now(jnp.dot(context, w_out, preferred_element_type=F32)) + bias_out
    )

    ln2, normed2, inv2 = layer_norm(middle, gain2, shift2)
    input2 = gather_now(ln2.astype(BF16))
    pre_act = jnp.dot(input2, w_fc, preferred_element_type=F32) + b_fc
    gelu_value, gelu_slope = gelu_pair(pre_act)
    activated = gelu_value.astype(BF16)
    grad_pre = contract(cot_low, w_proj, 1, 1) * gelu_slope
    grad_pre_low = grad_pre.astype(BF16)
    grad_in2 = scatter_now(contract(grad_pre_low, w_fc, 1, 1))
    output = (
        middle + scatter_group(jnp.dot(activated, w_proj, preferred_element_type=F32)) + bias_proj
    )
    grad_fc_bias = jnp.sum(grad_pre, axis=0)
    grad_proj_weight = contract(activated, cot_low, 0, 0)
    grad_fc_weight = contract(input2, grad_pre_low, 0, 0)

    def reduce_a(values, axes="a"):
        values = lax.psum_scatter(values.astype(BF16), axes, scatter_dimension=0, tiled=True)
        return lax.psum(values, "u") if n_u > 1 else values

    share_proj = lax.all_gather(reduce_a(grad_proj_weight), "v", axis=0, tiled=True).astype(F32)

    def columns_home(values):
        values = reduce_a(values).reshape(GB, depth, values.shape[1])
        values = lax.all_to_all(values, B_AXES, 0, 0, tiled=True)
        return lax.all_gather(values, "v", axis=0)

    share_fc = columns_home(grad_fc_weight).reshape(GV, GB, depth, n_a, half)
    share_fc = share_fc.transpose(2, 3, 1, 0, 4).reshape(depth, hidden).astype(F32)

    grad_gain2 = jnp.sum(grad_in2 * normed2, axis=0)
    grad_shift2 = jnp.sum(grad_in2, axis=0)
    grad_middle = cotangent + norm_back(grad_in2, normed2, inv2, gain2)

    mid_low = gather_now(grad_middle.astype(BF16))
    grad_out_weight = contract(context, mid_low, 0, 0)
    grad_context = contract(mid_low, w_out, 1, 1)
    grad_context = grad_context.astype(BF16).reshape(blocks, rows, heads_here, HEAD)
    grad_value = jnp.einsum("nhqk,nqhd->nkhd", probs_low, grad_context, preferred_element_type=F32)
    grad_probs = jnp.einsum("nqhd,nkhd->nhqk", grad_context, valued, preferred_element_type=F32)
    grad_scores = probs * (grad_probs - jnp.sum(probs * grad_probs, axis=-1, keepdims=True)) * scale
    grad_scores = grad_scores.astype(BF16)
    grad_query = jnp.einsum("nhqk,nkhd->nqhd", grad_scores, keyed, preferred_element_type=F32)
    grad_key = jnp.einsum("nhqk,nqhd->nkhd", grad_scores, query, preferred_element_type=F32)
    grad_query, grad_key, grad_value = (
        g.reshape(blocks * rows, cols) for g in (grad_query, grad_key, grad_value)
    )
    grad_query_bias = jnp.sum(grad_query, axis=0)
    grad_value_bias = jnp.sum(grad_value, axis=0)
    grad_qkv = jnp.concatenate([grad_query, grad_key, grad_value], axis=1).astype(BF16)
    grad_in1 = scatter_now(contract(grad_qkv, w_qkv, 1, 1))
    grad_qkv_weight = contract(input1, grad_qkv, 0, 0)

    share_qkv = columns_home(grad_qkv_weight).reshape(
        GV, n_bh, n_bl, depth, 3, heads_here, HEAD
    )
    share_qkv = share_qkv.transpose(3, 4, 2, 0, 5, 1, 6).reshape(depth, 3 * width).astype(F32)

    out_full = jnp.zeros((depth * n_a * n_bl, width), BF16)
    out_full = lax.dynamic_update_slice_in_dim(
        out_full, grad_out_weight.astype(BF16), slot * cols, 0
    )
    share_out = lax.psum(reduce_a(out_full, row_axes), "v").astype(F32)

    grad_gain1 = jnp.sum(grad_in1 * normed1, axis=0)
    grad_shift1 = jnp.sum(grad_in1, axis=0)
    tokens_grad = grad_middle + norm_back(grad_in1, normed1, inv1, gain1)

    def heads_full(values):
        here = (jnp.arange(GB * GV) == b * GV + v).astype(F32)
        values = here[:, None] * values[None, :]
        values = values.reshape(n_bh, n_bl, GV, heads_here, HEAD).transpose(1, 2, 3, 0, 4)
        return values.reshape(width)

    here = (jnp.arange(GB * GV) == b * GV + v).astype(F32)
    fc_full = here.reshape(1, GB, GV, 1) * grad_fc_bias.reshape(n_a, 1, 1, half)
    sums = [
        jnp.sum(cotangent, axis=0),
        grad_gain2,
        grad_shift2,
        jnp.sum(grad_middle, axis=0),
        heads_full(grad_query_bias),
        heads_full(grad_value_bias),
        grad_gain1,
        grad_shift1,
    ]
    sums = [s.reshape(shards, depth) for s in sums]
    sums = jnp.concatenate([*sums, fc_full.reshape(shards, hidden_rows)], axis=1)
    sums = sums_now(sums, n_u)
    (
        share_proj_bias,
        share_gain2,
        share_shift2,
        share_out_bias,
        share_query_bias,
        share_value_bias,
        share_gain1,
        share_shift1,
    ) = (sums[i * depth : (i + 1) * depth] for i in range(8))
    share_fc_bias = sums[8 * depth :]
    return (
        output,
        tokens_grad,
        share_gain1,
        share_shift1,
        share_qkv,
        share_query_bias,
        share_value_bias,
        share_out,
        share_out_bias,
        share_gain2,
        share_shift2,
        share_fc,
        share_fc_bias,
        share_proj,
        share_proj_bias,
    )


def solution(mesh):
    shard, replica = mesh.shape["shard"], mesh.shape["replica"]
    inner = Mesh(mesh.devices.reshape(shard // GB, 2, 2, replica // GV, GV), ALL_AXES)
    row = P(ALL_AXES, None)
    vec = P(S_AXES)
    mat = P(S_AXES, None)
    in_specs = (
        row, row, row, vec, vec, mat, vec, vec, mat, vec, vec, vec, mat, vec, mat, vec,
    )
    out_specs = (
        row, row, vec, vec, mat, vec, vec, mat, vec, vec, vec, mat, vec, mat, vec,
    )
    return jax.shard_map(
        on_device, mesh=inner, in_specs=in_specs, out_specs=out_specs, check_vma=False
    )
```

```python
import functools

import jax
import jax.numpy as jnp
from jax import lax
from jax.experimental import pallas as pl
from jax.experimental.pallas import tpu as pltpu
from jax.sharding import Mesh
from jax.sharding import PartitionSpec as P

HEADS = 16
HEAD = 64


EPS = 1e-05
GELU_C = 0.7978845608028654
GELU_A = 0.044715

GB = 4
GV = 2
G = GB * GV
B_AXES = ("b1", "b0")
G_AXES = ("b1", "b0", "v")
S_AXES = ("a", "b1", "b0")
ALL_AXES = ("a", "b1", "b0", "u", "v")
MESH = pl.DeviceIdType.MESH
VMEM = pl.BlockSpec(memory_space=pltpu.VMEM)
F32 = jnp.float32
BF16 = jnp.bfloat16


def layer_norm(values, gain, shift):
    row_mean = jnp.mean(values, axis=-1, keepdims=True)
    centered = values - row_mean
    inv_std = lax.rsqrt(jnp.mean(centered * centered, axis=-1, keepdims=True) + EPS)
    normed = centered * inv_std
    return (normed * gain + shift, normed, inv_std)


def norm_back(grad_out, normed, inv_std, gain):
    scaled = grad_out * gain
    return inv_std * (
        scaled
        - jnp.mean(scaled, axis=-1, keepdims=True)
        - normed * jnp.mean(scaled * normed, axis=-1, keepdims=True)
    )


def gelu_pair(pre_act):
    tangent = jnp.tanh(GELU_C * (pre_act + GELU_A * pre_act * pre_act * pre_act))
    value = 0.5 * pre_act * (1.0 + tangent)
    slope = 0.5 * (1.0 + tangent) + 0.5 * pre_act * (1.0 - tangent * tangent) * GELU_C * (
        1.0 + 3.0 * GELU_A * pre_act * pre_act
    )
    return (value, slope)


def contract(left, right, left_axis, right_axis):
    return lax.dot_general(
        left, right, (((left_axis,), (right_axis,)), ((), ())), preferred_element_type=F32
    )


def pick(values, index, axis):
    return lax.dynamic_index_in_dim(values, index, axis, keepdims=False)


def gather_group(values):
    return lax.all_gather(values, G_AXES, axis=0, tiled=True)


def scatter_group(values):
    return lax.psum_scatter(
        values.astype(BF16), G_AXES, scatter_dimension=0, tiled=True
    ).astype(F32)


def meet(peers):
    barrier = pltpu.get_barrier_semaphore()
    for peer in peers:
        pl.semaphore_signal(barrier, inc=1, device_id=peer, device_id_type=MESH)
    pl.semaphore_wait(barrier, len(peers))


def remote(src, dst, send, recv, peer):
    return pltpu.make_async_remote_copy(
        src_ref=src, dst_ref=dst, send_sem=send, recv_sem=recv, device_id=peer, device_id_type=MESH
    )


def group_place():
    b1, b0, v = (lax.axis_index(axis) for axis in G_AXES)
    chips = [((b1 + (d >> 1)) % 2, (v + (d & 1)) % 2) for d in range(4)]
    peers = [{"b1": c1, "b0": b0, "v": cv} for c1, cv in chips]
    partner = {"b1": b1, "b0": 1 - b0, "v": v}
    return b0, chips, peers, partner


def member(c1, b0, cv):
    return (c1 * 2 + b0) * GV + cv


def gather_kernel(x_ref, out_ref, send, recv, pass_send, pass_recv):
    b0, chips, peers, partner = group_place()
    mine = [member(c1, b0, cv) for c1, cv in chips]
    meet([partner, *peers[1:]])
    first = {}
    for d in (3, 1, 2, 0):
        first[d] = remote(
            x_ref, out_ref.at[mine[0]], send.at[d], recv.at[d], peers[d] if d else partner
        )
        first[d].start()
    out_ref[mine[0]] = x_ref[...]
    passed = []
    for d in (1, 2, 3):
        first[d].wait_recv()
        block = out_ref.at[mine[d]]
        copy = remote(block, block, pass_send.at[d - 1], pass_recv.at[d - 1], partner)
        copy.start()
        passed.append(copy)
    first[0].wait_recv()
    for copy in first.values():
        copy.wait_send()
    for copy in passed:
        copy.wait()


def scatter_kernel(
    y_ref, out_ref, came, total, arrived, send, recv, chip_send, chip_recv
):
    b0, chips, peers, partner = group_place()
    meet([partner, *peers[1:]])
    pair = {}
    for d in (3, 1, 2, 0):
        pair[d] = remote(
            y_ref.at[member(chips[d][0], 1 - b0, chips[d][1])],
            came.at[d],
            send.at[d],
            recv.at[d],
            partner,
        )
        pair[d].start()
    sent = {}
    for d in (3, 1, 2):
        pair[d].wait_recv()
        own = y_ref[member(chips[d][0], b0, chips[d][1])].astype(F32)
        total[d - 1] = (own + came[d].astype(F32)).astype(BF16)
        sent[d] = remote(
            total.at[d - 1], arrived.at[d - 1], chip_send.at[d - 1], chip_recv.at[d - 1], peers[d]
        )
        sent[d].start()
    pair[0].wait_recv()
    out_ref[...] = y_ref[member(chips[0][0], b0, chips[0][1])].astype(F32) + came[0].astype(F32)
    for d in (1, 2, 3):
        sent[d].wait_recv()
        out_ref[...] += arrived[d - 1].astype(F32)
    for d in range(4):
        pair[d].wait_send()
    for d in (1, 2, 3):
        sent[d].wait_send()


def call(kernel, out_shape, scratch, collective_id, cost, *args):
    many = isinstance(out_shape, tuple)
    return pl.pallas_call(
        kernel,
        out_shape=out_shape,
        in_specs=[VMEM] * len(args),
        out_specs=(VMEM,) * len(out_shape) if many else VMEM,
        scratch_shapes=scratch,
        cost_estimate=pl.CostEstimate(flops=0, bytes_accessed=cost, transcendentals=0),
        compiler_params=pltpu.CompilerParams(
            collective_id=collective_id, has_side_effects=True, vmem_limit_bytes=24 << 20
        ),
    )(*args)


def dma(n):
    return pltpu.SemaphoreType.DMA((n,))


def gather_now(values):
    rows, width = values.shape
    out = jax.ShapeDtypeStruct((G, rows, width), values.dtype)
    scratch = [dma(4), dma(4), dma(3), dma(3)]
    return call(gather_kernel, out, scratch, 0, 32 << 20, values).reshape(G * rows, width)


def scatter_now(values):
    rows, width = values.shape[0] // G, values.shape[1]
    block = (rows, width)
    scratch = [
        pltpu.VMEM((4, *block), BF16),
        pltpu.VMEM((3, *block), BF16),
        pltpu.VMEM((3, *block), BF16),
        dma(4),
        dma(4),
        dma(3),
        dma(3),
    ]
    out = jax.ShapeDtypeStruct(block, F32)
    return call(
        scatter_kernel, out, scratch, 1, 32 << 20, values.astype(BF16).reshape(G, *block)
    )


def shard_peers(shards):
    me = (lax.axis_index("a") * 2 + lax.axis_index("b1")) * 2 + lax.axis_index("b0")
    flats = [(me + k) % shards for k in range(shards)]
    peers = [{"a": f // GB, "b1": (f // 2) % 2, "b0": f % 2} for f in flats]
    return flats, peers


def group_peers():
    b1, b0, v = (lax.axis_index(axis) for axis in G_AXES)
    me = member(b1, b0, v)
    others = [(me + k) % G for k in range(G)]
    return others, [{"b1": o // 4, "b0": (o // 2) % 2, "v": o % 2} for o in others]


def start_kernel(
    shards,
    p_ref,
    s_ref,
    q_ref,
    f_ref,
    all_ref,
    seg_ref,
    q_all,
    f_all,
    send,
    recv,
    seg_send,
    seg_recv,
    q_send,
    q_recv,
    f_send,
    f_recv,
):
    flats, peers = shard_peers(shards)
    others, group = group_peers()
    me, mine = flats[0], others[0]
    b = me % GB
    columns = [(b + k) % GB for k in range(GB)]
    column_peers = [{"b1": o // 2, "b0": o % 2} for o in columns]
    meet([*peers[1:], *group[1:], *column_peers[1:]])
    copies = []
    for k in range(1, shards):
        copies.append(remote(p_ref, all_ref.at[me], send.at[k], recv.at[k], peers[k]))
        copies.append(
            remote(q_ref.at[flats[k] % GB], q_all.at[me], q_send.at[k], q_recv.at[k], peers[k])
        )
    for k in range(1, G):
        copies.append(remote(s_ref, seg_ref.at[mine], seg_send.at[k], seg_recv.at[k], group[k]))
    for k in range(1, GB):
        copies.append(
            remote(
                f_ref.at[columns[k]], f_all.at[b], f_send.at[k], f_recv.at[k], column_peers[k]
            )
        )
    for copy in copies:
        copy.start()
    all_ref[me] = p_ref[...]
    seg_ref[mine] = s_ref[...]
    q_all[me] = q_ref[b]
    f_all[b] = f_ref[b]
    for copy in copies:
        copy.wait()


def start_now(small, segments, qkv, fc, shards):
    small = small.astype(F32).reshape(-1, 128)
    segments = segments.astype(F32)
    out = (
        jax.ShapeDtypeStruct((shards, *small.shape), F32),
        jax.ShapeDtypeStruct((G, *segments.shape), F32),
        jax.ShapeDtypeStruct((shards, *qkv.shape[1:]), BF16),
        jax.ShapeDtypeStruct(fc.shape, BF16),
    )
    scratch = [dma(shards), dma(shards), dma(G), dma(G)]
    scratch += [dma(shards), dma(shards), dma(GB), dma(GB)]
    kernel = functools.partial(start_kernel, shards)
    params, segs, qkv, fc = call(kernel, out, scratch, 2, 32 << 20, small, segments, qkv, fc)
    return params.reshape(shards, -1), segs[:, 0], qkv, fc


def tail_kernel(
    shards,
    n_u,
    x_ref,
    q_ref,
    f_ref,
    p_ref,
    o_ref,
    x_out,
    q_out,
    f_out,
    p_out,
    o_out,
    came,
    total,
    extra,
    q_came,
    q_total,
    q_extra,
    send,
    recv,
    q_send,
    q_recv,
    f_send,
    f_recv,
    t_send,
    t_recv,
    one_send,
    one_recv,
):
    flats, peers = shard_peers(shards)
    others, group = group_peers()
    me, mine = flats[0], others[0]
    u, v = lax.axis_index("u"), lax.axis_index("v")
    b = me % GB
    twins_n = n_u * GV
    twins = [(u * GV + v + k) % twins_n for k in range(twins_n)]
    twins = [{"u": t // GV, "v": t % GV} for t in twins]
    other_v = {"v": 1 - v}
    meet([*peers[1:], *group[1:], *twins[1:], other_v])
    q_copies, copies, rest = [], [], []
    for k in range(1, shards):
        q_copies.append(
            remote(q_ref.at[flats[k]], q_came.at[k], q_send.at[k], q_recv.at[k], peers[k])
        )
        q_copies[-1].start()
    for k in range(1, shards):
        copies.append(remote(x_ref.at[flats[k]], came.at[k], send.at[k], recv.at[k], peers[k]))
        copies[-1].start()
    for k in range(1, G):
        to = others[k] // GV
        rest.append(
            remote(f_ref.at[to], f_out.at[v * GB + b], f_send.at[k], f_recv.at[k], group[k])
        )
    rest.append(remote(p_ref, p_out.at[v], one_send.at[0], one_recv.at[0], other_v))
    rest.append(remote(o_ref, o_out.at[v], one_send.at[1], one_recv.at[1], other_v))
    for copy in rest:
        copy.start()
    f_out[v * GB + b] = f_ref[b]
    p_out[v] = p_ref[...]
    o_out[v] = o_ref[...]

    for copy in q_copies:
        copy.wait_recv()
    for r in range(GB):
        start = q_ref[me].astype(F32) if r == 0 else q_came[r].astype(F32)
        for k in range(r + GB, shards, GB):
            start += q_came[k].astype(F32)
        q_total[(b + GB - r) % GB] = start.astype(BF16)
    value = x_ref[me]
    for k, copy in enumerate(copies, 1):
        copy.wait_recv()
        value += came[k]
    total[...] = value
    again = []
    for k in range(1, twins_n):
        pair = (
            remote(q_total, q_extra.at[k], t_send.at[k], t_recv.at[k], twins[k]),
            remote(
                total, extra.at[k], t_send.at[twins_n + k], t_recv.at[twins_n + k], twins[k]
            ),
        )
        for copy in pair:
            copy.start()
        again += pair
    for copy in again:
        copy.wait_recv()
    for k in range(1, twins_n):
        value += extra[k]
    x_out[...] = value
    for side in range(GV):
        first = q_total[...] if side == 0 else q_extra[side]
        first = first.astype(F32)
        for k in range(side + GV, twins_n, GV):
            first += q_extra[k].astype(F32)
        q_out[(v + side) % GV] = first
    for copy in rest:
        copy.wait()
    for copy in [*q_copies, *copies, *again]:
        copy.wait_send()


def tail_now(sums, qkv, fc, proj, out, n_u):
    shards, n = sums.shape
    sums = sums.reshape(shards, n // 128, 128)
    block, q_block = sums.shape[1:], qkv.shape[1:]
    twins_n = n_u * GV
    shapes = (
        jax.ShapeDtypeStruct(block, F32),
        jax.ShapeDtypeStruct((GV, GB, *q_block), F32),
        jax.ShapeDtypeStruct((GV * GB, *fc.shape[1:]), BF16),
        jax.ShapeDtypeStruct((GV, *proj.shape), BF16),
        jax.ShapeDtypeStruct((GV, *out.shape), BF16),
    )
    scratch = [
        pltpu.VMEM((shards, *block), F32),
        pltpu.VMEM(block, F32),
        pltpu.VMEM((twins_n, *block), F32),
        pltpu.VMEM((shards, *q_block), BF16),
        pltpu.VMEM((GB, *q_block), BF16),
        pltpu.VMEM((twins_n, GB, *q_block), BF16),
        *(dma(n) for n in (shards, shards, shards, shards, G, G)),
        *(dma(n) for n in (2 * twins_n, 2 * twins_n, 2, 2)),
    ]
    kernel = functools.partial(tail_kernel, shards, n_u)
    return call(kernel, shapes, scratch, 3, 32 << 20, sums, qkv, fc, proj, out)


def on_device(
    tokens,
    segment_ids,
    cotangent,
    norm1_gain,
    norm1_shift,
    qkv_weight,
    query_bias,
    value_bias,
    out_weight,
    out_bias,
    norm2_gain,
    norm2_shift,
    fc_weight,
    fc_bias,
    proj_weight,
    proj_bias,
):
    rows, width = tokens.shape
    n_a = lax.axis_size("a")
    n_u = lax.axis_size("u")
    shards = n_a * GB
    depth = width // shards
    n_bl = max(1, HEAD // depth)
    n_bh = GB // n_bl
    row_axes = ("a",) if n_bl == 1 else ("a", "b0")
    hidden_rows = fc_bias.shape[0]
    hidden = hidden_rows * shards
    half = hidden_rows // GV
    my_hidden = n_a * half
    heads_here = HEADS // (GB * GV)
    cols = heads_here * HEAD
    scale = HEAD ** (-0.5)
    v = lax.axis_index("v")
    b = lax.axis_index("b1") * 2 + lax.axis_index("b0")
    bl = b % n_bl

    small = jnp.concatenate(
        [
            norm1_gain,
            norm1_shift,
            query_bias,
            value_bias,
            out_bias,
            norm2_gain,
            norm2_shift,
            proj_bias,
            fc_bias,
        ]
    )
    def head_split(values):
        lead = values.shape[:-1]
        n = len(lead)
        values = values.reshape(*lead, n_bl, GV, heads_here, n_bh, HEAD)
        order = (n + 3, n, n + 1, *range(n), n + 2, n + 4)
        return values.transpose(order).reshape(n_bh, n_bl, GV, *lead, cols)

    qkv = pick(head_split(qkv_weight.reshape(depth, 3, width)), v, 2)
    qkv = qkv.reshape(GB, depth, 3 * cols)
    fc = pick(fc_weight.reshape(depth, n_a, GB, GV, half), v, 3)
    fc = fc.transpose(2, 0, 1, 3).reshape(GB, depth, my_hidden)
    small, segments, qkv, fc = start_now(small, segment_ids, qkv, fc, shards)
    gain1, shift1, bias_query, bias_value, bias_out, gain2, shift2, bias_proj = (
        small[:, i * depth : (i + 1) * depth].reshape(width) for i in range(8)
    )
    bias_fc = small[:, 8 * depth :]

    w_qkv = qkv.reshape(width, 3 * cols)
    w_out = lax.all_gather(out_weight, row_axes, axis=0, tiled=True)
    slot = bl * GV + v
    w_out = lax.dynamic_slice_in_dim(w_out, slot * cols, cols, 0)
    proj_half = lax.dynamic_slice_in_dim(proj_weight, v * half, half, 0)
    both = jnp.concatenate([fc.reshape(-1, width), proj_half], axis=0)
    both = lax.all_gather(both, "a", axis=0)
    w_fc = both[:, :-half].reshape(width, my_hidden)
    w_proj = both[:, -half:].reshape(my_hidden, width)

    def my_heads(values):
        return pick(head_split(values).reshape(GB, GV, cols), b, 0)

    bq = pick(my_heads(bias_query), v, 0)
    bv = pick(my_heads(bias_value), v, 0)
    b_fc = pick(pick(bias_fc.reshape(n_a, GB, GV, half), b, 1), v, 1).reshape(my_hidden)

    cot_low = gather_group(cotangent.astype(BF16))

    ln1, normed1, inv1 = layer_norm(tokens, gain1, shift1)
    input1 = gather_now(ln1.astype(BF16))
    blocks = GB * GV
    qkv_bias = jnp.concatenate([bq, jnp.zeros((cols,), F32), bv])
    projected = jnp.dot(input1, w_qkv, preferred_element_type=F32) + qkv_bias
    projected = projected.astype(BF16).reshape(blocks, rows, 3, heads_here, HEAD)
    query, keyed, valued = projected[:, :, 0], projected[:, :, 1], projected[:, :, 2]
    scores = jnp.einsum("nqhd,nkhd->nhqk", query, keyed, preferred_element_type=F32) * scale
    position = jnp.arange(rows)
    allowed = (segments[:, :, None] == segments[:, None, :]) & (
        position[None, :] <= position[:, None]
    )
    scores = jnp.where(allowed[:, None], scores, -1e30)
    top = jnp.max(scores, axis=-1, keepdims=True)
    log_total = top + jnp.log(jnp.sum(jnp.exp(scores - top), axis=-1, keepdims=True))
    probs = jnp.exp(scores - log_total)
    probs_low = probs.astype(BF16)
    context = jnp.einsum("nhqk,nkhd->nqhd", probs_low, valued, preferred_element_type=F32)
    context = context.reshape(blocks * rows, cols).astype(BF16)
    middle = (
        tokens + scatter_now(jnp.dot(context, w_out, preferred_element_type=F32)) + bias_out
    )

    ln2, normed2, inv2 = layer_norm(middle, gain2, shift2)
    input2 = gather_now(ln2.astype(BF16))
    pre_act = jnp.dot(input2, w_fc, preferred_element_type=F32) + b_fc
    gelu_value, gelu_slope = gelu_pair(pre_act)
    activated = gelu_value.astype(BF16)
    grad_pre = contract(cot_low, w_proj, 1, 1) * gelu_slope
    grad_pre_low = grad_pre.astype(BF16)
    grad_in2 = scatter_now(contract(grad_pre_low, w_fc, 1, 1))
    output = (
        middle + scatter_group(jnp.dot(activated, w_proj, preferred_element_type=F32)) + bias_proj
    )
    grad_fc_bias = jnp.sum(grad_pre, axis=0)
    grad_proj_weight = contract(activated, cot_low, 0, 0)
    grad_fc_weight = contract(input2, grad_pre_low, 0, 0)

    def reduce_a(values, axes="a"):
        values = lax.psum_scatter(values.astype(BF16), axes, scatter_dimension=0, tiled=True)
        return lax.psum(values, "u") if n_u > 1 else values

    part_proj = reduce_a(grad_proj_weight)
    part_fc = reduce_a(grad_fc_weight).reshape(GB, depth, my_hidden)

    grad_gain2 = jnp.sum(grad_in2 * normed2, axis=0)
    grad_shift2 = jnp.sum(grad_in2, axis=0)
    grad_middle = cotangent + norm_back(grad_in2, normed2, inv2, gain2)

    mid_low = gather_now(grad_middle.astype(BF16))
    grad_out_weight = contract(context, mid_low, 0, 0)
    grad_context = contract(mid_low, w_out, 1, 1)
    grad_context = grad_context.astype(BF16).reshape(blocks, rows, heads_here, HEAD)
    grad_value = jnp.einsum("nhqk,nqhd->nkhd", probs_low, grad_context, preferred_element_type=F32)
    grad_probs = jnp.einsum("nqhd,nkhd->nhqk", grad_context, valued, preferred_element_type=F32)
    grad_scores = probs * (grad_probs - jnp.sum(probs * grad_probs, axis=-1, keepdims=True)) * scale
    grad_scores = grad_scores.astype(BF16)
    grad_query = jnp.einsum("nhqk,nkhd->nqhd", grad_scores, keyed, preferred_element_type=F32)
    grad_key = jnp.einsum("nhqk,nqhd->nkhd", grad_scores, query, preferred_element_type=F32)
    grad_query, grad_key, grad_value = (
        g.reshape(blocks * rows, cols) for g in (grad_query, grad_key, grad_value)
    )
    grad_query_bias = jnp.sum(grad_query, axis=0)
    grad_value_bias = jnp.sum(grad_value, axis=0)
    grad_qkv = jnp.concatenate([grad_query, grad_key, grad_value], axis=1).astype(BF16)
    grad_in1 = scatter_now(contract(grad_qkv, w_qkv, 1, 1))
    grad_qkv_weight = contract(input1, grad_qkv, 0, 0)

    out_full = jnp.zeros((depth * n_a * n_bl, width), BF16)
    out_full = lax.dynamic_update_slice_in_dim(
        out_full, grad_out_weight.astype(BF16), slot * cols, 0
    )
    part_out = reduce_a(out_full, row_axes)

    grad_gain1 = jnp.sum(grad_in1 * normed1, axis=0)
    grad_shift1 = jnp.sum(grad_in1, axis=0)
    tokens_grad = grad_middle + norm_back(grad_in1, normed1, inv1, gain1)

    def heads_full(values):
        here = (jnp.arange(GB * GV) == b * GV + v).astype(F32)
        values = here[:, None] * values[None, :]
        values = values.reshape(n_bh, n_bl, GV, heads_here, HEAD).transpose(1, 2, 3, 0, 4)
        return values.reshape(width)

    here = (jnp.arange(GB * GV) == b * GV + v).astype(F32)
    fc_full = here.reshape(1, GB, GV, 1) * grad_fc_bias.reshape(n_a, 1, 1, half)
    sums = [
        jnp.sum(cotangent, axis=0),
        grad_gain2,
        grad_shift2,
        jnp.sum(grad_middle, axis=0),
        heads_full(grad_query_bias),
        heads_full(grad_value_bias),
        grad_gain1,
        grad_shift1,
    ]
    sums = [s.reshape(shards, depth) for s in sums]
    sums = jnp.concatenate([*sums, fc_full.reshape(shards, hidden_rows)], axis=1)
    part_qkv = grad_qkv_weight.astype(BF16).reshape(shards, depth, 3 * cols)
    sums, share_qkv, share_fc, share_proj, share_out = tail_now(
        sums, part_qkv, part_fc, part_proj, part_out, n_u
    )
    sums = sums.reshape(-1)
    share_qkv = share_qkv.reshape(GV, n_bh, n_bl, depth, 3, heads_here, HEAD)
    share_qkv = share_qkv.transpose(3, 4, 2, 0, 5, 1, 6).reshape(depth, 3 * width)
    share_fc = share_fc.reshape(GV, GB, depth, n_a, half)
    share_fc = share_fc.transpose(2, 3, 1, 0, 4).reshape(depth, hidden).astype(F32)
    share_proj = share_proj.reshape(hidden_rows, width).astype(F32)
    share_out = share_out[0].astype(F32) + share_out[1].astype(F32)
    (
        share_proj_bias,
        share_gain2,
        share_shift2,
        share_out_bias,
        share_query_bias,
        share_value_bias,
        share_gain1,
        share_shift1,
    ) = (sums[i * depth : (i + 1) * depth] for i in range(8))
    share_fc_bias = sums[8 * depth :]
    return (
        output,
        tokens_grad,
        share_gain1,
        share_shift1,
        share_qkv,
        share_query_bias,
        share_value_bias,
        share_out,
        share_out_bias,
        share_gain2,
        share_shift2,
        share_fc,
        share_fc_bias,
        share_proj,
        share_proj_bias,
    )


def solution(mesh):
    shard, replica = mesh.shape["shard"], mesh.shape["replica"]
    inner = Mesh(mesh.devices.reshape(shard // GB, 2, 2, replica // GV, GV), ALL_AXES)
    row = P(ALL_AXES, None)
    vec = P(S_AXES)
    mat = P(S_AXES, None)
    in_specs = (
        row, row, row, vec, vec, mat, vec, vec, mat, vec, vec, vec, mat, vec, mat, vec,
    )
    out_specs = (
        row, row, vec, vec, mat, vec, vec, mat, vec, vec, vec, mat, vec, mat, vec,
    )
    return jax.shard_map(
        on_device, mesh=inner, in_specs=in_specs, out_specs=out_specs, check_vma=False
    )
```

```python
import functools

import jax
import jax.numpy as jnp
from jax import lax
from jax.experimental import pallas as pl
from jax.experimental.pallas import tpu as pltpu
from jax.sharding import Mesh
from jax.sharding import PartitionSpec as P

HEADS = 16
HEAD = 64


EPS = 1e-05
GELU_C = 0.7978845608028654
GELU_A = 0.044715

GB = 4
GV = 2
G = GB * GV
B_AXES = ("b1", "b0")
G_AXES = ("b1", "b0", "v")
S_AXES = ("a", "b1", "b0")
ALL_AXES = ("a", "b1", "b0", "u", "v")
MESH = pl.DeviceIdType.MESH
VMEM = pl.BlockSpec(memory_space=pltpu.VMEM)
F32 = jnp.float32
BF16 = jnp.bfloat16


def layer_norm(values, gain, shift):
    row_mean = jnp.mean(values, axis=-1, keepdims=True)
    centered = values - row_mean
    inv_std = lax.rsqrt(jnp.mean(centered * centered, axis=-1, keepdims=True) + EPS)
    normed = centered * inv_std
    return (normed * gain + shift, normed, inv_std)


def norm_back(grad_out, normed, inv_std, gain):
    scaled = grad_out * gain
    return inv_std * (
        scaled
        - jnp.mean(scaled, axis=-1, keepdims=True)
        - normed * jnp.mean(scaled * normed, axis=-1, keepdims=True)
    )


def gelu_pair(pre_act):
    tangent = jnp.tanh(GELU_C * (pre_act + GELU_A * pre_act * pre_act * pre_act))
    value = 0.5 * pre_act * (1.0 + tangent)
    slope = 0.5 * (1.0 + tangent) + 0.5 * pre_act * (1.0 - tangent * tangent) * GELU_C * (
        1.0 + 3.0 * GELU_A * pre_act * pre_act
    )
    return (value, slope)


def contract(left, right, left_axis, right_axis):
    return lax.dot_general(
        left, right, (((left_axis,), (right_axis,)), ((), ())), preferred_element_type=F32
    )


def pick(values, index, axis):
    return lax.dynamic_index_in_dim(values, index, axis, keepdims=False)


def gather_group(values):
    return lax.all_gather(values, G_AXES, axis=0, tiled=True)


def meet(peers):
    barrier = pltpu.get_barrier_semaphore()
    for peer in peers:
        pl.semaphore_signal(barrier, inc=1, device_id=peer, device_id_type=MESH)
    pl.semaphore_wait(barrier, len(peers))


def remote(src, dst, send, recv, peer):
    return pltpu.make_async_remote_copy(
        src_ref=src, dst_ref=dst, send_sem=send, recv_sem=recv, device_id=peer, device_id_type=MESH
    )


def group_place():
    b1, b0, v = (lax.axis_index(axis) for axis in G_AXES)
    chips = [((b1 + (d >> 1)) % 2, (v + (d & 1)) % 2) for d in range(4)]
    peers = [{"b1": c1, "b0": b0, "v": cv} for c1, cv in chips]
    partner = {"b1": b1, "b0": 1 - b0, "v": v}
    return b0, chips, peers, partner


def member(c1, b0, cv):
    return (c1 * 2 + b0) * GV + cv


def gather_kernel(x_ref, out_ref, send, recv, pass_send, pass_recv):
    b0, chips, peers, partner = group_place()
    mine = [member(c1, b0, cv) for c1, cv in chips]
    meet([partner, *peers[1:]])
    first = {}
    for d in (3, 1, 2, 0):
        first[d] = remote(
            x_ref, out_ref.at[mine[0]], send.at[d], recv.at[d], peers[d] if d else partner
        )
        first[d].start()
    out_ref[mine[0]] = x_ref[...]
    passed = []
    for d in (1, 2, 3):
        first[d].wait_recv()
        block = out_ref.at[mine[d]]
        copy = remote(block, block, pass_send.at[d - 1], pass_recv.at[d - 1], partner)
        copy.start()
        passed.append(copy)
    first[0].wait_recv()
    for copy in first.values():
        copy.wait_send()
    for copy in passed:
        copy.wait()


def scatter_kernel(
    y_ref, out_ref, came, total, arrived, send, recv, chip_send, chip_recv
):
    b0, chips, peers, partner = group_place()
    meet([partner, *peers[1:]])
    pair = {}
    for d in (3, 1, 2, 0):
        pair[d] = remote(
            y_ref.at[member(chips[d][0], 1 - b0, chips[d][1])],
            came.at[d],
            send.at[d],
            recv.at[d],
            partner,
        )
        pair[d].start()
    sent = {}
    for d in (3, 1, 2):
        pair[d].wait_recv()
        own = y_ref[member(chips[d][0], b0, chips[d][1])].astype(F32)
        total[d - 1] = (own + came[d].astype(F32)).astype(BF16)
        sent[d] = remote(
            total.at[d - 1], arrived.at[d - 1], chip_send.at[d - 1], chip_recv.at[d - 1], peers[d]
        )
        sent[d].start()
    pair[0].wait_recv()
    out_ref[...] = y_ref[member(chips[0][0], b0, chips[0][1])].astype(F32) + came[0].astype(F32)
    for d in (1, 2, 3):
        sent[d].wait_recv()
        out_ref[...] += arrived[d - 1].astype(F32)
    for d in range(4):
        pair[d].wait_send()
    for d in (1, 2, 3):
        sent[d].wait_send()


def call(kernel, out_shape, scratch, collective_id, cost, *args):
    many = isinstance(out_shape, tuple)
    return pl.pallas_call(
        kernel,
        out_shape=out_shape,
        in_specs=[VMEM] * len(args),
        out_specs=(VMEM,) * len(out_shape) if many else VMEM,
        scratch_shapes=scratch,
        cost_estimate=pl.CostEstimate(flops=0, bytes_accessed=cost, transcendentals=0),
        compiler_params=pltpu.CompilerParams(
            collective_id=collective_id, has_side_effects=True, vmem_limit_bytes=24 << 20
        ),
    )(*args)


def dma(n):
    return pltpu.SemaphoreType.DMA((n,))


def gather_now(values):
    rows, width = values.shape
    out = jax.ShapeDtypeStruct((G, rows, width), values.dtype)
    scratch = [dma(4), dma(4), dma(3), dma(3)]
    return call(gather_kernel, out, scratch, 0, 32 << 20, values).reshape(G * rows, width)


def scatter_now(values):
    rows, width = values.shape[0] // G, values.shape[1]
    block = (rows, width)
    scratch = [
        pltpu.VMEM((4, *block), BF16),
        pltpu.VMEM((3, *block), BF16),
        pltpu.VMEM((3, *block), BF16),
        dma(4),
        dma(4),
        dma(3),
        dma(3),
    ]
    out = jax.ShapeDtypeStruct(block, F32)
    return call(
        scatter_kernel, out, scratch, 1, 32 << 20, values.astype(BF16).reshape(G, *block)
    )


def shard_peers(shards):
    me = (lax.axis_index("a") * 2 + lax.axis_index("b1")) * 2 + lax.axis_index("b0")
    flats = [(me + k) % shards for k in range(shards)]
    peers = [{"a": f // GB, "b1": (f // 2) % 2, "b0": f % 2} for f in flats]
    return flats, peers


def group_peers():
    b1, b0, v = (lax.axis_index(axis) for axis in G_AXES)
    me = member(b1, b0, v)
    others = [(me + k) % G for k in range(G)]
    return others, [{"b1": o // 4, "b0": (o // 2) % 2, "v": o % 2} for o in others]


def start_kernel(
    shards,
    n_bl,
    p_ref,
    s_ref,
    q_ref,
    f_ref,
    o_ref,
    all_ref,
    seg_ref,
    q_all,
    f_all,
    o_all,
    send,
    recv,
    seg_send,
    seg_recv,
    q_send,
    q_recv,
    f_send,
    f_recv,
    o_send,
    o_recv,
):
    flats, peers = shard_peers(shards)
    others, group = group_peers()
    me, mine = flats[0], others[0]
    b = me % GB
    row_n = shards // GB * n_bl
    b0 = lax.axis_index("b0")
    row = lax.axis_index("a") * n_bl + b0 % n_bl
    row_ids = [(row + k) % row_n for k in range(row_n)]
    row_peers = [{"a": r // n_bl, "b0": r % n_bl if n_bl > 1 else b0} for r in row_ids]
    columns = [(b + k) % GB for k in range(GB)]
    column_peers = [{"b1": o // 2, "b0": o % 2} for o in columns]
    meet([*peers[1:], *group[1:], *column_peers[1:]])
    copies = []
    for k in range(1, shards):
        copies.append(remote(p_ref, all_ref.at[me], send.at[k], recv.at[k], peers[k]))
        copies.append(
            remote(q_ref.at[flats[k] % GB], q_all.at[me], q_send.at[k], q_recv.at[k], peers[k])
        )
    for k in range(1, G):
        copies.append(remote(s_ref, seg_ref.at[mine], seg_send.at[k], seg_recv.at[k], group[k]))
    for k in range(1, GB):
        copies.append(
            remote(
                f_ref.at[columns[k]], f_all.at[b], f_send.at[k], f_recv.at[k], column_peers[k]
            )
        )
    for k in range(1, row_n):
        copies.append(remote(o_ref, o_all.at[row], o_send.at[k], o_recv.at[k], row_peers[k]))
    for copy in copies:
        copy.start()
    o_all[row] = o_ref[...]
    all_ref[me] = p_ref[...]
    seg_ref[mine] = s_ref[...]
    q_all[me] = q_ref[b]
    f_all[b] = f_ref[b]
    for copy in copies:
        copy.wait()


def start_now(small, segments, qkv, fc, out_weight, shards, n_bl):
    small = small.astype(F32).reshape(-1, 128)
    segments = segments.astype(F32)
    out = (
        jax.ShapeDtypeStruct((shards, *small.shape), F32),
        jax.ShapeDtypeStruct((G, *segments.shape), F32),
        jax.ShapeDtypeStruct((shards, *qkv.shape[1:]), BF16),
        jax.ShapeDtypeStruct(fc.shape, BF16),
        jax.ShapeDtypeStruct((shards // GB * n_bl, *out_weight.shape), BF16),
    )
    scratch = [dma(shards), dma(shards), dma(G), dma(G)]
    scratch += [dma(shards), dma(shards), dma(GB), dma(GB), dma(shards), dma(shards)]
    kernel = functools.partial(start_kernel, shards, n_bl)
    params, segs, qkv, fc, rows = call(
        kernel, out, scratch, 2, 32 << 20, small, segments, qkv, fc, out_weight
    )
    return params.reshape(shards, -1), segs[:, 0], qkv, fc, rows


def tail_kernel(
    shards,
    n_u,
    x_ref,
    q_ref,
    f_ref,
    p_ref,
    o_ref,
    x_out,
    q_out,
    f_out,
    p_out,
    o_out,
    came,
    total,
    extra,
    q_came,
    q_total,
    q_extra,
    send,
    recv,
    q_send,
    q_recv,
    f_send,
    f_recv,
    t_send,
    t_recv,
    one_send,
    one_recv,
):
    flats, peers = shard_peers(shards)
    others, group = group_peers()
    me, mine = flats[0], others[0]
    u, v = lax.axis_index("u"), lax.axis_index("v")
    b = me % GB
    twins_n = n_u * GV
    twins = [(u * GV + v + k) % twins_n for k in range(twins_n)]
    twins = [{"u": t // GV, "v": t % GV} for t in twins]
    other_v = {"v": 1 - v}
    meet([*peers[1:], *group[1:], *twins[1:], other_v])
    q_copies, copies, rest = [], [], []
    for k in range(1, shards):
        q_copies.append(
            remote(q_ref.at[flats[k]], q_came.at[k], q_send.at[k], q_recv.at[k], peers[k])
        )
        q_copies[-1].start()
    for k in range(1, shards):
        copies.append(remote(x_ref.at[flats[k]], came.at[k], send.at[k], recv.at[k], peers[k]))
        copies[-1].start()
    for k in range(1, G):
        to = others[k] // GV
        rest.append(
            remote(f_ref.at[to], f_out.at[v * GB + b], f_send.at[k], f_recv.at[k], group[k])
        )
    rest.append(remote(p_ref, p_out.at[v], one_send.at[0], one_recv.at[0], other_v))
    rest.append(remote(o_ref, o_out.at[v], one_send.at[1], one_recv.at[1], other_v))
    for copy in rest:
        copy.start()
    f_out[v * GB + b] = f_ref[b]
    p_out[v] = p_ref[...]
    o_out[v] = o_ref[...]

    for copy in q_copies:
        copy.wait_recv()
    for r in range(GB):
        start = q_ref[me].astype(F32) if r == 0 else q_came[r].astype(F32)
        for k in range(r + GB, shards, GB):
            start += q_came[k].astype(F32)
        q_total[(b + GB - r) % GB] = start.astype(BF16)
    value = x_ref[me]
    for k, copy in enumerate(copies, 1):
        copy.wait_recv()
        value += came[k]
    total[...] = value
    again = []
    for k in range(1, twins_n):
        pair = (
            remote(q_total, q_extra.at[k], t_send.at[k], t_recv.at[k], twins[k]),
            remote(
                total, extra.at[k], t_send.at[twins_n + k], t_recv.at[twins_n + k], twins[k]
            ),
        )
        for copy in pair:
            copy.start()
        again += pair
    for copy in again:
        copy.wait_recv()
    for k in range(1, twins_n):
        value += extra[k]
    x_out[...] = value
    for side in range(GV):
        first = q_total[...] if side == 0 else q_extra[side]
        first = first.astype(F32)
        for k in range(side + GV, twins_n, GV):
            first += q_extra[k].astype(F32)
        q_out[(v + side) % GV] = first.astype(BF16)
    for copy in rest:
        copy.wait()
    for copy in [*q_copies, *copies, *again]:
        copy.wait_send()


def tail_now(sums, qkv, fc, proj, out, n_u):
    shards, n = sums.shape
    sums = sums.reshape(shards, n // 128, 128)
    block, q_block = sums.shape[1:], qkv.shape[1:]
    twins_n = n_u * GV
    shapes = (
        jax.ShapeDtypeStruct(block, F32),
        jax.ShapeDtypeStruct((GV, GB, *q_block), BF16),
        jax.ShapeDtypeStruct((GV * GB, *fc.shape[1:]), BF16),
        jax.ShapeDtypeStruct((GV, *proj.shape), BF16),
        jax.ShapeDtypeStruct((GV, *out.shape), BF16),
    )
    scratch = [
        pltpu.VMEM((shards, *block), F32),
        pltpu.VMEM(block, F32),
        pltpu.VMEM((twins_n, *block), F32),
        pltpu.VMEM((shards, *q_block), BF16),
        pltpu.VMEM((GB, *q_block), BF16),
        pltpu.VMEM((twins_n, GB, *q_block), BF16),
        *(dma(n) for n in (shards, shards, shards, shards, G, G)),
        *(dma(n) for n in (2 * twins_n, 2 * twins_n, 2, 2)),
    ]
    kernel = functools.partial(tail_kernel, shards, n_u)
    return call(kernel, shapes, scratch, 3, 32 << 20, sums, qkv, fc, proj, out)


def on_device(
    tokens,
    segment_ids,
    cotangent,
    norm1_gain,
    norm1_shift,
    qkv_weight,
    query_bias,
    value_bias,
    out_weight,
    out_bias,
    norm2_gain,
    norm2_shift,
    fc_weight,
    fc_bias,
    proj_weight,
    proj_bias,
):
    rows, width = tokens.shape
    n_a = lax.axis_size("a")
    n_u = lax.axis_size("u")
    shards = n_a * GB
    depth = width // shards
    n_bl = max(1, HEAD // depth)
    n_bh = GB // n_bl
    row_axes = ("a",) if n_bl == 1 else ("a", "b0")
    hidden_rows = fc_bias.shape[0]
    hidden = hidden_rows * shards
    half = hidden_rows // GV
    my_hidden = n_a * half
    heads_here = HEADS // (GB * GV)
    cols = heads_here * HEAD
    scale = HEAD ** (-0.5)
    v = lax.axis_index("v")
    b = lax.axis_index("b1") * 2 + lax.axis_index("b0")
    bl = b % n_bl

    small = jnp.concatenate(
        [
            norm1_gain,
            norm1_shift,
            query_bias,
            value_bias,
            out_bias,
            norm2_gain,
            norm2_shift,
            proj_bias,
            fc_bias,
        ]
    )
    def head_split(values):
        lead = values.shape[:-1]
        n = len(lead)
        values = values.reshape(*lead, n_bl, GV, heads_here, n_bh, HEAD)
        order = (n + 3, n, n + 1, *range(n), n + 2, n + 4)
        return values.transpose(order).reshape(n_bh, n_bl, GV, *lead, cols)

    qkv = pick(head_split(qkv_weight.reshape(depth, 3, width)), v, 2)
    qkv = qkv.reshape(GB, depth, 3 * cols)
    fc = pick(fc_weight.reshape(depth, n_a, GB, GV, half), v, 3)
    fc = fc.transpose(2, 0, 1, 3).reshape(GB, depth, my_hidden)
    small, segments, qkv, fc, w_out = start_now(
        small, segment_ids, qkv, fc, out_weight, shards, n_bl
    )
    gain1, shift1, bias_query, bias_value, bias_out, gain2, shift2, bias_proj = (
        small[:, i * depth : (i + 1) * depth].reshape(width) for i in range(8)
    )
    bias_fc = small[:, 8 * depth :]

    w_qkv = qkv.reshape(width, 3 * cols)
    w_out = w_out.reshape(-1, width)
    slot = bl * GV + v
    w_out = lax.dynamic_slice_in_dim(w_out, slot * cols, cols, 0)
    proj_half = lax.dynamic_slice_in_dim(proj_weight, v * half, half, 0)
    both = jnp.concatenate([fc.reshape(-1, width), proj_half], axis=0)
    both = lax.all_gather(both, "a", axis=0)
    w_fc = both[:, :-half].reshape(width, my_hidden)
    w_proj = both[:, -half:].reshape(my_hidden, width)

    def my_heads(values):
        return pick(head_split(values).reshape(GB, GV, cols), b, 0)

    bq = pick(my_heads(bias_query), v, 0)
    bv = pick(my_heads(bias_value), v, 0)
    b_fc = pick(pick(bias_fc.reshape(n_a, GB, GV, half), b, 1), v, 1).reshape(my_hidden)

    cot_low = gather_group(cotangent.astype(BF16))

    ln1, normed1, inv1 = layer_norm(tokens, gain1, shift1)
    input1 = gather_now(ln1.astype(BF16))
    blocks = GB * GV
    qkv_bias = jnp.concatenate([bq, jnp.zeros((cols,), F32), bv])
    projected = jnp.dot(input1, w_qkv, preferred_element_type=F32) + qkv_bias
    projected = projected.astype(BF16).reshape(blocks, rows, 3, heads_here, HEAD)
    query, keyed, valued = projected[:, :, 0], projected[:, :, 1], projected[:, :, 2]
    scores = jnp.einsum("nqhd,nkhd->nhqk", query, keyed, preferred_element_type=F32) * scale
    position = jnp.arange(rows)
    allowed = (segments[:, :, None] == segments[:, None, :]) & (
        position[None, :] <= position[:, None]
    )
    scores = jnp.where(allowed[:, None], scores, -1e30)
    top = jnp.max(scores, axis=-1, keepdims=True)
    log_total = top + jnp.log(jnp.sum(jnp.exp(scores - top), axis=-1, keepdims=True))
    probs = jnp.exp(scores - log_total)
    probs_low = probs.astype(BF16)
    context = jnp.einsum("nhqk,nkhd->nqhd", probs_low, valued, preferred_element_type=F32)
    context = context.reshape(blocks * rows, cols).astype(BF16)
    middle = (
        tokens + scatter_now(jnp.dot(context, w_out, preferred_element_type=F32)) + bias_out
    )

    ln2, normed2, inv2 = layer_norm(middle, gain2, shift2)
    input2 = gather_now(ln2.astype(BF16))
    pre_act = jnp.dot(input2, w_fc, preferred_element_type=F32) + b_fc
    gelu_value, gelu_slope = gelu_pair(pre_act)
    activated = gelu_value.astype(BF16)
    grad_pre = contract(cot_low, w_proj, 1, 1) * gelu_slope
    grad_pre_low = grad_pre.astype(BF16)
    grad_in2 = scatter_now(contract(grad_pre_low, w_fc, 1, 1))
    output = (
        middle + scatter_now(jnp.dot(activated, w_proj, preferred_element_type=F32)) + bias_proj
    )
    grad_fc_bias = jnp.sum(grad_pre, axis=0)
    grad_proj_weight = contract(activated, cot_low, 0, 0)
    grad_fc_weight = contract(input2, grad_pre_low, 0, 0)

    def reduce_a(values, axes="a"):
        values = lax.psum_scatter(values.astype(BF16), axes, scatter_dimension=0, tiled=True)
        return lax.psum(values, "u") if n_u > 1 else values

    part_proj = reduce_a(grad_proj_weight)
    part_fc = reduce_a(grad_fc_weight).reshape(GB, depth, my_hidden)

    grad_gain2 = jnp.sum(grad_in2 * normed2, axis=0)
    grad_shift2 = jnp.sum(grad_in2, axis=0)
    grad_middle = cotangent + norm_back(grad_in2, normed2, inv2, gain2)

    mid_low = gather_now(grad_middle.astype(BF16))
    grad_out_weight = contract(context, mid_low, 0, 0)
    grad_context = contract(mid_low, w_out, 1, 1)
    grad_context = grad_context.astype(BF16).reshape(blocks, rows, heads_here, HEAD)
    grad_value = jnp.einsum("nhqk,nqhd->nkhd", probs_low, grad_context, preferred_element_type=F32)
    grad_probs = jnp.einsum("nqhd,nkhd->nhqk", grad_context, valued, preferred_element_type=F32)
    grad_scores = probs * (grad_probs - jnp.sum(probs * grad_probs, axis=-1, keepdims=True)) * scale
    grad_scores = grad_scores.astype(BF16)
    grad_query = jnp.einsum("nhqk,nkhd->nqhd", grad_scores, keyed, preferred_element_type=F32)
    grad_key = jnp.einsum("nhqk,nqhd->nkhd", grad_scores, query, preferred_element_type=F32)
    grad_query, grad_key, grad_value = (
        g.reshape(blocks * rows, cols) for g in (grad_query, grad_key, grad_value)
    )
    grad_query_bias = jnp.sum(grad_query, axis=0)
    grad_value_bias = jnp.sum(grad_value, axis=0)
    grad_qkv = jnp.concatenate([grad_query, grad_key, grad_value], axis=1).astype(BF16)
    grad_in1 = scatter_now(contract(grad_qkv, w_qkv, 1, 1))
    grad_qkv_weight = contract(input1, grad_qkv, 0, 0)

    out_full = jnp.zeros((depth * n_a * n_bl, width), BF16)
    out_full = lax.dynamic_update_slice_in_dim(
        out_full, grad_out_weight.astype(BF16), slot * cols, 0
    )
    part_out = reduce_a(out_full, row_axes)

    grad_gain1 = jnp.sum(grad_in1 * normed1, axis=0)
    grad_shift1 = jnp.sum(grad_in1, axis=0)
    tokens_grad = grad_middle + norm_back(grad_in1, normed1, inv1, gain1)

    def heads_full(values):
        here = (jnp.arange(GB * GV) == b * GV + v).astype(F32)
        values = here[:, None] * values[None, :]
        values = values.reshape(n_bh, n_bl, GV, heads_here, HEAD).transpose(1, 2, 3, 0, 4)
        return values.reshape(width)

    here = (jnp.arange(GB * GV) == b * GV + v).astype(F32)
    fc_full = here.reshape(1, GB, GV, 1) * grad_fc_bias.reshape(n_a, 1, 1, half)
    sums = [
        jnp.sum(cotangent, axis=0),
        grad_gain2,
        grad_shift2,
        jnp.sum(grad_middle, axis=0),
        heads_full(grad_query_bias),
        heads_full(grad_value_bias),
        grad_gain1,
        grad_shift1,
    ]
    sums = [s.reshape(shards, depth) for s in sums]
    sums = jnp.concatenate([*sums, fc_full.reshape(shards, hidden_rows)], axis=1)
    part_qkv = grad_qkv_weight.astype(BF16).reshape(shards, depth, 3 * cols)
    sums, share_qkv, share_fc, share_proj, share_out = tail_now(
        sums, part_qkv, part_fc, part_proj, part_out, n_u
    )
    sums = sums.reshape(-1)
    share_qkv = share_qkv.reshape(GV, n_bh, n_bl, depth, 3, heads_here, HEAD)
    share_qkv = share_qkv.transpose(3, 4, 2, 0, 5, 1, 6).reshape(depth, 3 * width).astype(F32)
    share_fc = share_fc.reshape(GV, GB, depth, n_a, half)
    share_fc = share_fc.transpose(2, 3, 1, 0, 4).reshape(depth, hidden).astype(F32)
    share_proj = share_proj.reshape(hidden_rows, width).astype(F32)
    share_out = share_out[0].astype(F32) + share_out[1].astype(F32)
    (
        share_proj_bias,
        share_gain2,
        share_shift2,
        share_out_bias,
        share_query_bias,
        share_value_bias,
        share_gain1,
        share_shift1,
    ) = (sums[i * depth : (i + 1) * depth] for i in range(8))
    share_fc_bias = sums[8 * depth :]
    return (
        output,
        tokens_grad,
        share_gain1,
        share_shift1,
        share_qkv,
        share_query_bias,
        share_value_bias,
        share_out,
        share_out_bias,
        share_gain2,
        share_shift2,
        share_fc,
        share_fc_bias,
        share_proj,
        share_proj_bias,
    )


def solution(mesh):
    shard, replica = mesh.shape["shard"], mesh.shape["replica"]
    inner = Mesh(mesh.devices.reshape(shard // GB, 2, 2, replica // GV, GV), ALL_AXES)
    row = P(ALL_AXES, None)
    vec = P(S_AXES)
    mat = P(S_AXES, None)
    in_specs = (
        row, row, row, vec, vec, mat, vec, vec, mat, vec, vec, vec, mat, vec, mat, vec,
    )
    out_specs = (
        row, row, vec, vec, mat, vec, vec, mat, vec, vec, vec, mat, vec, mat, vec,
    )
    return jax.shard_map(
        on_device, mesh=inner, in_specs=in_specs, out_specs=out_specs, check_vma=False
    )
```
